512 devices in a mesh: wa: 16 (over x, z_lo, core), gx: 32 (over z_hi, y).
Axes of the slice: x: 4, y: 8, z: 8 (z_hi: 4, z_lo: 2; z = z_hi * 2 + z_lo), core: 2. Of those that a mesh axis runs over, the one named last changes fastest.
Arguments:
- part_pos: float32 [3, 32, 128, 128], P(None, 'wa', 'gx'), may hold values from 0 to 32, as said below
- part_vel: float32 [3, 32, 128, 128], P(None, 'wa', 'gx'), may hold values from -6 to 6
- random_kicks: float32 [4, 32, 128, 128], P(None, 'wa', 'gx'), may hold values from -5 to 5
- vert_pos: float32 [3, 512, 498], P(None, ('wa', 'gx')), may hold values from -3 to 128
- vert_vel: float32 [3, 512, 498], P(None, ('wa', 'gx')), may hold values from -6 to 6
- cover_start: int32 [512], P('wa'), may hold values from 0 to 29, as said below
- bond_ends: int32 [1488, 2], replicated, may hold values from 0 to 497, as said below
- triangles: int32 [992, 3], replicated, may hold values from 0 to 497, as said below
- rest_len: float32 [1488], replicated, may hold values from 1 to 3
- rest_area: float32 [992], replicated, may hold values from 0.5 to 3
Outputs:
- final_part_pos: float32 [3, 32, 128, 128], P(None, 'wa', 'gx')
- final_part_vel: float32 [3, 32, 128, 128], P(None, 'wa', 'gx')
- final_vert_pos: float32 [3, 512, 498], P(None, ('wa', 'gx'))
- final_vert_vel: float32 [3, 512, 498], P(None, ('wa', 'gx'))
The draws below stay inside these ranges and needn't reach their ends.
Inputs may be any that keep to these rules, and one draw needn't show every extreme that they name: `part_pos`: components 0 and 1 lie in [0, 1), component 2 in [0, 32). `cover_start`: A cell's covered slabs may lie anywhere along its row, far from the slab that holds it. In every row some slab is covered by exactly 5 cells and none by more. `bond_ends`: the two vertices of a bond differ. `triangles`: the three vertices of a triangle differ.
All inputs are finite; a program needn't handle non-finite values.
Results may differ from the reference program's by a relative error of at most 0.0003.
Values sent between devices are 32-bit elements; how exact they have to be, the bound alone decides.
No kernel may reach another device: no remote copies, remote signals or barrier semaphores. Data moves between devices by JAX's collectives and lax.ppermute only.
A program may use at most 64 MiB of HBM per device.

```python
import math
import jax
import jax.numpy as jnp
from jax import lax

TW = 2
TF = 4
TPART = 128
HEIGHT = 32
NV = 498
CELLS_DEV = 1
SPAN = 3
STEPS = 2
NB = 1488
NT = 992
MAXCOV = 5
ROWS_W = 16
SLABS_F = 32
NW = 32
NF = 128
CELLS_ROW = 32
CELLS = 512


def cover_table(key):
    row_keys = jax.random.split(jax.random.fold_in(key, 11), ROWS_W)

    def one_row(row_key):
        back_key, hot_key, place_key = jax.random.split(row_key, 3)
        places = jax.random.permutation(place_key, jnp.arange(CELLS_ROW, dtype=jnp.int32)) // CELLS_DEV
        backward = jax.random.randint(back_key, (CELLS_ROW,), 0, 3)
        hottest = jax.random.randint(hot_key, (), 2, SLABS_F - 2)
        relative = places - hottest
        nearby = (relative >= -2) & (relative <= 2)
        start_hot = places - 1 - jnp.floor_divide(relative, 2)
        start_any = jnp.where(nearby, start_hot, places - backward)
        return jnp.clip(start_any, 0, SLABS_F - SPAN)
    return jax.vmap(one_row)(row_keys).reshape(-1).astype(jnp.int32)


def draw_cover_start(key, part):
    return cover_table(key)


def draw_vert_pos(key, part):
    starts = cover_table(key).astype(jnp.float32)
    sub_keys = jax.random.split(jax.random.fold_in(key, 23), 4)
    direction = jax.random.normal(sub_keys[0], (3, CELLS, NV), jnp.float32)
    direction = direction / jnp.sqrt(jnp.sum(direction * direction, 0, keepdims=True) + 1e-06)
    radius = 2.0
    jitter_size = 0.1
    jitter = jax.random.uniform(sub_keys[1], (3, CELLS, NV), jnp.float32, -jitter_size, jitter_size)
    centre_w = 0.5 * TW + jax.random.uniform(sub_keys[2], (CELLS,), jnp.float32, -0.3, 0.3)
    centre_f = (starts + 0.5 * SPAN) * TF
    centre_z = jax.random.uniform(sub_keys[3], (CELLS,), jnp.float32, 3.0, HEIGHT - 3.0)
    centre = jnp.stack([centre_w, centre_f, centre_z])[:, :, None]
    return centre + radius * direction + jitter


def draw_part_pos(key, part):
    sub_keys = jax.random.split(jax.random.fold_in(key, 5), 2)
    inplane = jax.random.uniform(sub_keys[0], (2, NW, NF, TPART), jnp.float32)
    height = jax.random.uniform(sub_keys[1], (1, NW, NF, TPART), jnp.float32, 0.0, HEIGHT)
    return jnp.concatenate([inplane, height], 0)


def draw_bond_ends(key, part):
    sub_keys = jax.random.split(jax.random.fold_in(key, 31), 2)
    leading = jax.random.randint(sub_keys[0], (NB,), 0, NV)
    offset = jax.random.randint(sub_keys[1], (NB,), 1, NV)
    return jnp.stack([leading, (leading + offset) % NV], 1).astype(jnp.int32)


def draw_triangles(key, part):
    sub_keys = jax.random.split(jax.random.fold_in(key, 37), 3)
    leading = jax.random.randint(sub_keys[0], (NT,), 0, NV)
    step_one = jax.random.randint(sub_keys[1], (NT,), 1, NV - 1)
    step_two = jax.random.randint(sub_keys[2], (NT,), 1, NV - step_one)
    return jnp.stack([leading, (leading + step_one) % NV, (leading + step_one + step_two) % NV], 1).astype(jnp.int32)


def levels(rng, dims, shards, least, largest):
    gain = 1.0
    for position, shards_of in shards:
        steps = jax.random.uniform(jax.random.fold_in(jax.random.fold_in(rng, 6), position), (shards_of,), jnp.float32, least / len(shards), largest / len(shards))
        gain = gain * jnp.repeat(jnp.exp(steps), dims[position] // shards_of).reshape((-1,) + (1,) * (len(dims) - 1 - position))
    return gain


def centred(stream_key, shape, spread, reach, cuts=(), kind=jnp.bfloat16):
    loudness = levels(stream_key, shape, cuts, -0.22, 0.18) if cuts else 1.0
    result = jax.random.normal(stream_key, shape, jnp.float32) * spread * loudness
    return jnp.minimum(jnp.maximum(result, -reach), reach).astype(kind)


def setup_inputs(seed: int = 0) -> dict:
    seeds = jax.random.split(jax.random.key(seed), 11)
    return {
        "part_pos": draw_part_pos(jax.random.fold_in(seeds[10], 71), 0),
        "part_vel": centred(seeds[1], (3, NW, NF, TPART), 1.0, 6.0, ((1, 16), (2, 32)), jnp.float32),
        "random_kicks": centred(seeds[2], (2 * STEPS, NW, NF, TPART), 1.0, 5.0, ((1, 16), (2, 32)), jnp.float32),
        "vert_pos": draw_vert_pos(jax.random.fold_in(seeds[10], 71), 0),
        "vert_vel": centred(seeds[4], (3, CELLS, NV), 1.0, 6.0, ((1, 512),), jnp.float32),
        "cover_start": draw_cover_start(jax.random.fold_in(seeds[10], 71), 0),
        "bond_ends": draw_bond_ends(jax.random.fold_in(seeds[10], 71), 0),
        "triangles": draw_triangles(jax.random.fold_in(seeds[10], 71), 0),
        "rest_len": jnp.clip(jnp.exp(jax.random.uniform(seeds[8], (NB,), jnp.float32, math.log(1.0), math.log(3.0))), 1.0, 3.0),
        "rest_area": jnp.clip(jnp.exp(jax.random.uniform(seeds[9], (NT,), jnp.float32, math.log(0.5), math.log(3.0))), 0.5, 3.0),
    }


TIME_STEP = 0.04
SOLVENT_REPULSION = 25.0
SOLVENT_FRICTION = 4.5
NOISE_SCALE = 15.0
MEMBRANE_REPULSION = 4.0
MEMBRANE_FRICTION = 4.5
BOND_STIFFNESS = 2.0
AREA_STIFFNESS = 0.5
HALF_ROOT = 0.7071067811865476

def solvent_terms(own_part, near_part, shift_w, shift_f, near_mask):
    delta_w = own_part[0][:, :, None] - near_part[0][:, None, :] - shift_w
    delta_f = own_part[1][:, :, None] - near_part[1][:, None, :] - shift_f
    delta_z = own_part[2][:, :, None] - near_part[2][:, None, :]
    speed_w = own_part[3][:, :, None] - near_part[3][:, None, :]
    speed_f = own_part[4][:, :, None] - near_part[4][:, None, :]
    speed_z = own_part[5][:, :, None] - near_part[5][:, None, :]
    theta_pair = (own_part[6][:, :, None] * near_part[7][:, None, :] + own_part[7][:, :, None] * near_part[6][:, None, :]) * HALF_ROOT
    weight = jnp.maximum(1.0 - (delta_w * delta_w + delta_f * delta_f + delta_z * delta_z), 0.0) * near_mask[:, None, None]
    scalar = SOLVENT_REPULSION * weight - SOLVENT_FRICTION * weight * weight * (delta_w * speed_w + delta_f * speed_f + delta_z * speed_z) + NOISE_SCALE * weight * theta_pair
    return jnp.stack([lax.optimization_barrier(jnp.sum(scalar * delta_w, 2)), lax.optimization_barrier(jnp.sum(scalar * delta_f, 2)), lax.optimization_barrier(jnp.sum(scalar * delta_z, 2))])

def couple_cell(part_frame, part_speed, cell_frame, cell_speed, cell_weight):
    delta_w = part_frame[0][None, :] - cell_frame[0][:, None]
    delta_f = part_frame[1][None, :] - cell_frame[1][:, None]
    delta_z = part_frame[2][None, :] - cell_frame[2][:, None]
    speed_w = part_speed[0][None, :] - cell_speed[0][:, None]
    speed_f = part_speed[1][None, :] - cell_speed[1][:, None]
    speed_z = part_speed[2][None, :] - cell_speed[2][:, None]
    weight = jnp.maximum(1.0 - (delta_w * delta_w + delta_f * delta_f + delta_z * delta_z), 0.0) * cell_weight
    scalar = MEMBRANE_REPULSION * weight - MEMBRANE_FRICTION * weight * weight * (delta_w * speed_w + delta_f * speed_f + delta_z * speed_z)
    push_w = scalar * delta_w
    push_f = scalar * delta_f
    push_z = scalar * delta_z
    on_parts = jnp.stack([lax.optimization_barrier(jnp.sum(push_w, 0)), lax.optimization_barrier(jnp.sum(push_f, 0)), lax.optimization_barrier(jnp.sum(push_z, 0))])
    on_cell = -jnp.stack([lax.optimization_barrier(jnp.sum(push_w, 1)), lax.optimization_barrier(jnp.sum(push_f, 1)), lax.optimization_barrier(jnp.sum(push_z, 1))])
    return (on_parts, on_cell)

def slab_coupling(part_frame, part_speed, row_frame, row_speed, starts, slab_id):
    cell_count = starts.shape[0]
    order_ids = jnp.arange(cell_count, dtype=jnp.int32)
    covered = (starts <= slab_id) & (slab_id < starts + SPAN)
    sort_key = jnp.where(covered, 0, cell_count).astype(jnp.int32) + order_ids
    chosen = jnp.argsort(sort_key)[:MAXCOV].astype(jnp.int32)
    weights = covered[chosen].astype(jnp.float32)
    cell_frames = jnp.moveaxis(row_frame[:, chosen], 1, 0)
    cell_speeds = jnp.moveaxis(row_speed[:, chosen], 1, 0)

    def visit(running, member):
        cell_frame, cell_speed, cell_weight = member
        on_parts, on_cell = couple_cell(part_frame, part_speed, cell_frame, cell_speed, cell_weight)
        return (running + on_parts, on_cell)
    summed, pushes = lax.scan(visit, jnp.zeros(part_frame.shape, jnp.float32), (cell_frames, cell_speeds, weights))
    one_hot = (chosen[:, None] == order_ids[None, :]).astype(jnp.float32)
    reaction = jnp.einsum('mr,mcv->crv', one_hot, pushes, precision=lax.Precision.HIGHEST)
    return (summed, reaction)

def slab_frame(tile_pos, base_f):
    tiles_w = tile_pos.shape[1]
    tiles_f = tile_pos.shape[2]
    along_w = jnp.arange(tiles_w, dtype=jnp.int32).astype(jnp.float32)[:, None, None]
    along_f = (base_f + jnp.arange(tiles_f, dtype=jnp.int32)).astype(jnp.float32)[None, :, None]
    framed = jnp.stack([tile_pos[0] + along_w, tile_pos[1] + along_f, tile_pos[2]])
    return framed.reshape(3, -1)

def bond_energy(positions, bond_ends, triangles, rest_len, rest_area):
    bond_head = positions[:, :, bond_ends[:, 0]]
    bond_tail = positions[:, :, bond_ends[:, 1]]
    stretch = lax.optimization_barrier(jnp.sum((bond_head - bond_tail) ** 2, 0))
    sq_len = rest_len * rest_len
    energy = 0.25 * BOND_STIFFNESS * jnp.sum((stretch - sq_len) ** 2 / sq_len)
    corner_one = positions[:, :, triangles[:, 0]]
    corner_two = positions[:, :, triangles[:, 1]]
    corner_three = positions[:, :, triangles[:, 2]]
    edge_one = corner_two - corner_one
    edge_two = corner_three - corner_one
    normal_w = edge_one[1] * edge_two[2] - edge_one[2] * edge_two[1]
    normal_f = edge_one[2] * edge_two[0] - edge_one[0] * edge_two[2]
    normal_z = edge_one[0] * edge_two[1] - edge_one[1] * edge_two[0]
    area_sq = 0.25 * (normal_w * normal_w + normal_f * normal_f + normal_z * normal_z)
    sq_area = rest_area * rest_area
    return energy + 0.25 * AREA_STIFFNESS * jnp.sum((area_sq - sq_area) ** 2 / sq_area)

def bond_force(positions, bond_ends, triangles, rest_len, rest_area):
    return -jax.grad(bond_energy)(positions, bond_ends, triangles, rest_len, rest_area)

def solvent_force(bundle):
    padded = jnp.pad(bundle, ((0, 0), (1, 1), (1, 1), (0, 0)))
    inside = jnp.pad(jnp.ones((NW, NF), jnp.float32), 1)

    def one_row(tile_row):
        own_part = lax.dynamic_index_in_dim(bundle, tile_row, 1, keepdims=False)
        running_sum = jnp.zeros((3, NF, TPART), jnp.float32)
        for off_w in (-1, 0, 1):
            line_near = lax.dynamic_index_in_dim(padded, tile_row + 1 + off_w, 1, keepdims=False)
            line_mask = lax.dynamic_index_in_dim(inside, tile_row + 1 + off_w, 0, keepdims=False)
            for off_f in (-1, 0, 1):
                near_part = line_near[:, 1 + off_f:1 + off_f + NF]
                running_sum = running_sum + solvent_terms(own_part, near_part, float(off_w), float(off_f), line_mask[1 + off_f:1 + off_f + NF])
        return running_sum
    row_forces = lax.map(one_row, jnp.arange(NW, dtype=jnp.int32))
    return jnp.transpose(row_forces, (1, 0, 2, 3))

def membrane_all(part_pos, part_vel, vert_pos, vert_vel, cover_start):
    zero_index = jnp.zeros((), jnp.int32)

    def slab_job(slab_id):
        row_id = slab_id // SLABS_F
        col_id = slab_id % SLABS_F
        tile_pos = lax.dynamic_slice(part_pos, (zero_index, row_id * TW, col_id * TF, zero_index), (3, TW, TF, TPART))
        tile_vel = lax.dynamic_slice(part_vel, (zero_index, row_id * TW, col_id * TF, zero_index), (3, TW, TF, TPART))
        row_frame = lax.dynamic_slice_in_dim(vert_pos, row_id * CELLS_ROW, CELLS_ROW, 1)
        row_speed = lax.dynamic_slice_in_dim(vert_vel, row_id * CELLS_ROW, CELLS_ROW, 1)
        starts = lax.dynamic_slice_in_dim(cover_start, row_id * CELLS_ROW, CELLS_ROW, 0)
        summed, reaction = slab_coupling(slab_frame(tile_pos, col_id * TF), tile_vel.reshape(3, -1), row_frame, row_speed, starts, col_id)
        return (summed.reshape(3, TW, TF, TPART), reaction)
    groups = jnp.arange(ROWS_W * SLABS_F, dtype=jnp.int32).reshape(-1, 4)
    forces, reactions = lax.map(jax.vmap(slab_job), groups)
    forces = forces.reshape(ROWS_W, SLABS_F, 3, TW, TF, TPART)
    forces = jnp.transpose(forces, (2, 0, 3, 1, 4, 5)).reshape(3, NW, NF, TPART)
    reactions = lax.optimization_barrier(jnp.sum(reactions.reshape(ROWS_W, SLABS_F, 3, CELLS_ROW, NV), 1))
    reactions = jnp.transpose(reactions, (1, 0, 2, 3)).reshape(3, CELLS, NV)
    return (forces, reactions)

def reference(part_pos, part_vel, random_kicks, vert_pos, vert_vel, cover_start, bond_ends, triangles, rest_len, rest_area):
    for step_index in range(STEPS):
        bundle = jnp.concatenate([part_pos, part_vel, random_kicks[2 * step_index:2 * step_index + 2]], 0)
        solvent = solvent_force(bundle)
        membrane, reaction = membrane_all(part_pos, part_vel, vert_pos, vert_vel, cover_start)
        bonded = bond_force(vert_pos, bond_ends, triangles, rest_len, rest_area)
        vert_vel = vert_vel + TIME_STEP * (reaction + bonded)
        vert_pos = vert_pos + TIME_STEP * vert_vel
        part_vel = part_vel + TIME_STEP * (solvent + membrane)
        part_pos = part_pos + TIME_STEP * part_vel
    return (part_pos, part_vel, vert_pos, vert_vel)
```

```python
import functools

import jax
import jax.numpy as jnp
from jax import lax
from jax.experimental import pallas as pl
from jax.experimental.pallas import tpu as pltpu
from jax.sharding import PartitionSpec as P

SPAN = 3
MAXCOV = 5
DT = 0.04
FAR = 1000.0
ZMID = 16.0
NOISE = 15.0 * 0.7071067811865476
TW = 2
TF = 4
LANES = 128
NV = 498
NVP = 512
NB = 1488
NBP = 1536
NT = 992
NTP = 1024
COLS = NBP + 2 * NTP
SLABS = 32
ROWS = 16

F32 = jnp.float32
BF16 = jnp.bfloat16


def nn(a, b):
    return lax.dot_general(a, b, (((1,), (0,)), ((), ())), preferred_element_type=F32)


def nt(a, b):
    return lax.dot_general(a, b, (((1,), (1,)), ((), ())), preferred_element_type=F32)


def split3(x):
    a = x.astype(BF16).astype(F32)
    r = x - a
    b = r.astype(BF16).astype(F32)
    return a, b, r - b


def row_ids(n):
    return lax.broadcasted_iota(jnp.int32, (8, n), 0)


def rows_of(pieces, n):
    row = row_ids(n)
    out = jnp.zeros((8, n), F32)
    for r, piece in pieces:
        out = jnp.where(row == r, piece, out)
    return out


def dots(st, n):
    row = row_ids(n)
    vel = pltpu.roll(st, 5, 0)
    sq = jnp.sum(jnp.where(row < 3, st * st, 0.0), 0, keepdims=True)
    xv = jnp.sum(jnp.where(row < 3, st * vel, 0.0), 0, keepdims=True)
    return vel, sq, xv


def left_features(st):
    n = st.shape[1]
    a, b, c = split3(st)
    _, sq, xv = dots(st, n)
    s1, s2, s3 = split3(1.0 - sq)
    v1, v2, v3 = split3(xv)
    e1 = rows_of([(0, s1), (1, s2), (2, s3), (3, v1), (4, v2), (5, v3), (6, 1.0), (7, 1.0)], n)
    e2 = rows_of([(0, 1.0)], n)
    return jnp.concatenate([a, a, a, b, b, c, e1, e2], 0)


def right_features(st):
    n = st.shape[1]
    row = row_ids(n)
    vel, sq, xv = dots(st, n)
    s1, s2, s3 = split3(-sq)
    v1, v2, v3 = split3(4.5 * xv)

    def pack(block, e1, e2):
        a, b, c = split3(block)
        return jnp.concatenate([a, b, c, a, b, a, e1, e2], 0).astype(BF16)

    zero = jnp.zeros((8, n), F32)
    near = pack(
        jnp.where(row < 3, 2.0 * st, 0.0),
        rows_of([(0, 1.0), (1, 1.0), (2, 1.0), (6, s1), (7, s2)], n),
        rows_of([(0, s3)], n),
    )
    pos = pltpu.roll(st, 3, 0)
    drag = pack(
        -4.5 * jnp.where(row < 3, vel, jnp.where(row < 6, pos, 0.0)),
        rows_of([(3, 4.5), (4, 4.5), (5, 4.5), (6, v1), (7, v2)], n),
        rows_of([(0, v3)], n),
    )
    up = pltpu.roll(st, 7, 0)
    down = pltpu.roll(st, 1, 0)
    kick = pack(
        NOISE * jnp.where(row == 6, up, jnp.where(row == 7, down, 0.0)),
        rows_of([(6, 25.0)], n),
        zero,
    )
    return near, drag, kick


def sum_features(st):
    n = st.shape[1]
    row = row_ids(n)
    q = jnp.where(row < 3, st, jnp.where(row == 3, 1.0, 0.0))
    a, b, c = split3(q)
    return jnp.concatenate([a, b, c, jnp.zeros((8, n), F32)], 0).astype(BF16)


def halves(s):
    hi = s.astype(BF16)
    return hi, (s - hi.astype(F32)).astype(BF16)


def moment(acc):
    return acc[0:8] + acc[8:16] + acc[16:24]


def cover_slots(starts, j, idx, slot_map, count_ref):
    for m in range(8):
        idx[m] = 0
    count = jnp.int32(0)
    shifts = (-2, -1, 1, 2)
    counts = [jnp.int32(0) for _ in shifts]
    for c in range(SLABS):
        s = starts[c]
        idx[jnp.minimum(count, 7)] = c
        covered = (s <= j) & (j < s + SPAN)
        count = count + covered.astype(jnp.int32)
        if slot_map is not None:
            for k, shift in enumerate(shifts):
                slot_map[k * SLABS + c] = jnp.minimum(counts[k], 7)
                cov = (s <= j + shift) & (j + shift < s + SPAN)
                counts[k] = counts[k] + cov.astype(jnp.int32)
    count = jnp.minimum(count, MAXCOV)
    count_ref[0] = count
    return count


def bond_force(pos, m_ref, rest_len, rest_area):
    p3 = jnp.concatenate(split3(pos), 0).astype(BF16)

    def fold(x):
        return x[0:24] + x[24:48] + x[48:72]

    def back(g, cols):
        g3 = jnp.concatenate(split3(g), 0).astype(BF16)
        return fold(nt(g3, m_ref[:, cols]))

    one, two, three = slice(0, NBP), slice(NBP, NBP + NTP), slice(NBP + NTP, COLS)
    d = fold(nn(p3, m_ref[:, one]))
    sq_len = rest_len * rest_len
    stretch = d[0:8] * d[0:8] + d[8:16] * d[8:16] + d[16:24] * d[16:24]
    coef = (stretch - sq_len) * (-2.0 / sq_len)
    force = back(jnp.concatenate([coef * d[0:8], coef * d[8:16], coef * d[16:24]], 0), one)
    e1 = fold(nn(p3, m_ref[:, two]))
    e2 = fold(nn(p3, m_ref[:, three]))

    def cross(a, b):
        ax, ay, az = a
        bx, by, bz = b
        return ay * bz - az * by, az * bx - ax * bz, ax * by - ay * bx

    a = (e1[0:8], e1[8:16], e1[16:24])
    b = (e2[0:8], e2[8:16], e2[16:24])
    n = cross(a, b)
    sq_area = rest_area * rest_area
    area = 0.25 * (n[0] * n[0] + n[1] * n[1] + n[2] * n[2])
    coef = (area - sq_area) * (-0.125 / sq_area)
    g = (coef * n[0], coef * n[1], coef * n[2])
    force = force + back(jnp.concatenate(cross(b, g), 0), two)
    return force + back(jnp.concatenate(cross(g, a), 0), three)


def particle_frames(i, j, own, wl, wh, gl, gh):
    row = row_ids(LANES)

    def framed(tile, w, f, bad):
        shift = jnp.where(row == 2, -ZMID, 0.0)
        shift = jnp.where(row == 0, w + bad, shift)
        shift = jnp.where(row == 1, f, shift)
        return tile + shift

    wlo = jnp.where(i == 0, FAR, 0.0)
    whi = jnp.where(i == ROWS - 1, FAR, 0.0)
    flo = jnp.where(j == 0, FAR, 0.0)
    fhi = jnp.where(j == SLABS - 1, FAR, 0.0)
    near = []
    for w in range(TW + 2):
        bad_w = wlo if w == 0 else whi if w == TW + 1 else 0.0
        for f in range(TF + 2):
            if f == 0:
                tile, bad = gl[w], bad_w + flo
            elif f == TF + 1:
                tile, bad = gh[w], bad_w + fhi
            elif w == 0:
                tile, bad = wl[0, f - 1], bad_w
            elif w == TW + 1:
                tile, bad = wh[0, f - 1], bad_w
            else:
                tile, bad = own[w - 1, f - 1], 0.0
            near.append(framed(tile, float(w - 1), float(f - 1), bad))
    return near


def forces(near, count, cs, ms, lfeat, lcell, rnear, rdrag, qown, fpart, fcell):
    nst = jnp.concatenate(near, 1)
    own_tiles = [near[(w + 1) * (TF + 2) + f + 1] for w in range(TW) for f in range(TF)]
    own = jnp.concatenate(own_tiles, 1)
    ra, rc, rb = right_features(own)
    rnear[...] = ra
    rdrag[...] = rc
    qown[...] = sum_features(own)
    lfeat[...] = left_features(nst).T.astype(BF16)
    qnear = sum_features(nst)
    for w in range(TW):
        for f in range(TF):
            t = w * TF + f
            cols = slice(t * LANES, (t + 1) * LANES)
            rt = jnp.concatenate([ra[:, cols], rc[:, cols], rb[:, cols]], 1)
            acc = jnp.zeros((32, LANES), F32)
            for dw in range(3):
                first = ((w + dw) * (TF + 2) + f) * LANES
                out = nn(lfeat[first : first + 3 * LANES, :], rt)
                weight = jnp.maximum(out[:, :LANES], 0.0)
                s = weight * (out[:, 2 * LANES :] - weight * out[:, LANES : 2 * LANES])
                hi, lo = halves(s)
                q = qnear[:, first : first + 3 * LANES]
                acc = acc + nn(q, hi) + nn(q, lo)
            fpart[:, cols] = acc

    def one_cell(m, carry):
        st = cs[m]
        lcell[...] = left_features(st).T.astype(BF16)
        q = sum_features(st)
        total = jnp.zeros((32, NVP), F32)
        for k in range(4):
            cols = slice(k * 256, (k + 1) * 256)
            weight = jnp.maximum(nn(lcell[...], rnear[:, cols]), 0.0)
            s = weight * (4.0 - weight * nn(lcell[...], rdrag[:, cols]))
            hi, lo = halves(s)
            fpart[:, cols] += nn(q, hi) + nn(q, lo)
            qo = qown[:, cols]
            total = total + nt(qo, hi) + nt(qo, lo)
        fcell[m] = total
        return carry

    lax.fori_loop(0, count, one_cell, 0)
    return own


def move_particles(own_refs, fpart, own, store):
    mom = moment(fpart[...])
    force = own * mom[3:4] - mom
    n = own.shape[1]
    row = row_ids(n)
    kick = pltpu.roll(jnp.where(row < 3, DT * force, 0.0), 3, 0)
    for w in range(TW):
        for f in range(TF):
            t = w * TF + f
            st = own_refs[w, f] + kick[:, t * LANES : (t + 1) * LANES]
            vel = pltpu.roll(st, 5, 0)
            st = st + jnp.where(row_ids(LANES) < 3, DT * vel, 0.0)
            store(w, f, st)


def first_kernel(
    starts, own, wl, wh, gl, gh, kicks, cells, hi_ids, lo_ids, rest_len, rest_area,
    out_t, out_c, out_r, m_ref,
    idx, cnt, cs, ps, lfeat, lcell, rnear, rdrag, qown, fpart, fcell,
):
    i = lax.axis_index("wa")
    j = lax.axis_index("gx")
    count = cover_slots(starts, j, idx, None, cnt)
    for k in range(COLS // 512):
        cols = slice(k * 512, (k + 1) * 512)
        vid = lax.broadcasted_iota(jnp.int32, (NVP, 512), 0)
        plus = (vid == hi_ids[:, cols]).astype(F32)
        minus = (vid == lo_ids[:, cols]).astype(F32)
        m_ref[:, cols] = (plus - minus).astype(BF16)
    ps[...] = jnp.zeros((48, NVP), F32)
    row = row_ids(NVP)
    shift = jnp.where(row == 1, -(j * TF).astype(F32), jnp.where(row == 2, -ZMID, 0.0))
    away = jnp.where(row < 3, FAR, 0.0)
    for m in range(MAXCOV):
        st = jnp.where(m < count, cells[idx[m]] + shift, away)
        cs[m] = st
        for c in range(6):
            ps[c * 8 + m : c * 8 + m + 1, :] = st[c : c + 1, :]
    near = particle_frames(i, j, own, wl, wh, gl, gh)
    fcell[...] = jnp.zeros(fcell.shape, F32)
    own_st = forces(near, count, cs, None, lfeat, lcell, rnear, rdrag, qown, fpart, fcell)

    def store(w, f, st):
        out_t[w, f, 0:6, :] = st[0:6]
        out_t[w, f, 6:8, :] = kicks[w, f]

    move_particles(own, fpart, own_st, store)
    out_r[...] = jnp.zeros((24, NVP), F32)
    for m in range(MAXCOV):
        mom = moment(fcell[m])
        react = DT * (cs[m] * mom[3:4] - mom)
        for c in range(3):
            out_r[c * 8 + m : c * 8 + m + 1, :] = react[c : c + 1, :]
    bond = bond_force(ps[0:24, :], m_ref, rest_len[...], rest_area[...])
    out_c[0:24, :] = ps[0:24, :]
    out_c[24:48, :] = ps[24:48, :] + DT * bond + out_r[...]


def second_kernel(
    starts, own, wl, wh, gl, gh, cst, r0, r1, r2, r3, m_ref, rest_len, rest_area,
    out_t, out_s,
    idx, cnt, smap, cs, ps, lfeat, lcell, rnear, rdrag, qown, fpart, fcell,
):
    i = lax.axis_index("wa")
    j = lax.axis_index("gx")
    count = cover_slots(starts, j, idx, smap, cnt)
    ps[...] = cst[...]
    for m in range(MAXCOV):
        cell = idx[m]
        s = starts[cell]
        for k, (shift, ref) in enumerate(((-2, r0), (-1, r1), (1, r2), (2, r3))):
            slot = smap[k * SLABS + cell]
            there = (m < count) & (s <= j + shift) & (j + shift < s + SPAN)
            for c in range(3):
                at = 24 + c * 8 + m
                got = ref[pl.ds(c * 8 + slot, 1), :]
                ps[at : at + 1, :] += jnp.where(there, got, 0.0)
    ps[0:24, :] += DT * ps[24:48, :]
    for m in range(MAXCOV):
        cs[m] = jnp.zeros((8, NVP), F32)
        for c in range(6):
            cs[m, c : c + 1, :] = ps[c * 8 + m : c * 8 + m + 1, :]
    near = particle_frames(i, j, own, wl, wh, gl, gh)
    fcell[...] = jnp.zeros(fcell.shape, F32)
    own_st = forces(near, count, cs, None, lfeat, lcell, rnear, rdrag, qown, fpart, fcell)

    def store(w, f, st):
        out_t[w, f] = st

    move_particles(own, fpart, own_st, store)
    bond = bond_force(ps[0:24, :], m_ref, rest_len[...], rest_area[...])
    ps[24:48, :] += DT * bond
    out_s[...] = jnp.zeros(out_s.shape, F32)
    row = row_ids(NVP)
    shift = jnp.where(row == 1, (j * TF).astype(F32), jnp.where(row == 2, ZMID, 0.0))
    for m in range(MAXCOV):
        cell = idx[m]
        mom = moment(fcell[m])
        react = DT * (cs[m] * mom[3:4] - mom)
        share = pltpu.roll(jnp.where(row < 3, react, 0.0), 3, 0)
        for c in range(6):
            cs[m, c : c + 1, :] = ps[c * 8 + m : c * 8 + m + 1, :]
        whole = jnp.where(starts[cell] == j, cs[m] + shift, 0.0)

        @pl.when(m < count)
        def _():
            out_s[cell] = whole + share


def vmem():
    return pl.BlockSpec(memory_space=pltpu.VMEM)


def smem():
    return pl.BlockSpec(memory_space=pltpu.SMEM)


def common_scratch():
    return [
        pltpu.VMEM((8, 8, NVP), F32),
        pltpu.VMEM((48, NVP), F32),
        pltpu.VMEM((24 * LANES, 64), BF16),
        pltpu.VMEM((NVP, 64), BF16),
        pltpu.VMEM((64, 8 * LANES), BF16),
        pltpu.VMEM((64, 8 * LANES), BF16),
        pltpu.VMEM((32, 8 * LANES), BF16),
        pltpu.VMEM((32, 8 * LANES), F32),
        pltpu.VMEM((8, 32, NVP), F32),
    ]


def moves(axis, shift):
    count = lax.axis_size(axis)
    return [(k, k + shift) for k in range(count) if 0 <= k + shift < count]


def halo(tiles):
    wl = lax.ppermute(tiles[TW - 1 :], "wa", moves("wa", 1))
    wh = lax.ppermute(tiles[:1], "wa", moves("wa", -1))
    last = jnp.concatenate([wl[:, TF - 1], tiles[:, TF - 1], wh[:, TF - 1]], 0)
    head = jnp.concatenate([wl[:, 0], tiles[:, 0], wh[:, 0]], 0)
    gl = lax.ppermute(last, "gx", moves("gx", 1))
    gh = lax.ppermute(head, "gx", moves("gx", -1))
    return wl, wh, gl, gh


def body(
    part_pos, part_vel, random_kicks, vert_pos, vert_vel,
    cover_start, bond_ends, triangles, rest_len, rest_area,
):
    tiles = jnp.transpose(
        jnp.concatenate([part_pos, part_vel, random_kicks[0:2]], 0), (1, 2, 0, 3)
    )
    kicks = jnp.transpose(random_kicks[2:4], (1, 2, 0, 3))
    heads = [bond_ends[:, 0], triangles[:, 1], triangles[:, 2]]
    tails = [bond_ends[:, 1], triangles[:, 0], triangles[:, 0]]
    sizes = [NBP, NTP, NTP]

    def lay(parts):
        return jnp.concatenate(
            [jnp.pad(p, (0, n - p.shape[0]), constant_values=-1) for p, n in zip(parts, sizes)]
        )[None]

    hi_ids, lo_ids = lay(heads), lay(tails)
    rl = jnp.pad(rest_len, (0, NBP - NB), constant_values=1.0)[None]
    ra = jnp.pad(rest_area, (0, NTP - NT), constant_values=1.0)[None]
    cell = jnp.concatenate(
        [
            jnp.pad(vert_pos[:, 0], ((0, 0), (0, NVP - NV)), constant_values=FAR),
            jnp.pad(vert_vel[:, 0], ((0, 2), (0, NVP - NV))),
        ],
        0,
    )
    cells = lax.all_to_all(
        jnp.broadcast_to(cell[None], (SLABS, 8, NVP)), "gx", 0, 0, tiled=True
    )
    shape = jax.ShapeDtypeStruct
    wl, wh, gl, gh = halo(tiles)
    new_tiles, cst, share, incidence = pl.pallas_call(
        first_kernel,
        out_shape=(
            shape((TW, TF, 8, LANES), F32),
            shape((48, NVP), F32),
            shape((24, NVP), F32),
            shape((NVP, COLS), BF16),
        ),
        in_specs=[smem()] + [vmem()] * 11,
        out_specs=tuple([vmem()] * 4),
        scratch_shapes=[pltpu.SMEM((8,), jnp.int32), pltpu.SMEM((1,), jnp.int32)]
        + common_scratch(),
        name="first_step",
    )(cover_start, tiles, wl, wh, gl, gh, kicks, cells, hi_ids, lo_ids, rl, ra)
    got = [lax.ppermute(share, "gx", moves("gx", -s)) for s in (-2, -1, 1, 2)]
    wl, wh, gl, gh = halo(new_tiles)
    last_tiles, sends = pl.pallas_call(
        second_kernel,
        out_shape=(shape((TW, TF, 8, LANES), F32), shape((SLABS, 8, NVP), F32)),
        in_specs=[smem()] + [vmem()] * 13,
        out_specs=(vmem(), vmem()),
        scratch_shapes=[
            pltpu.SMEM((8,), jnp.int32),
            pltpu.SMEM((1,), jnp.int32),
            pltpu.SMEM((4 * SLABS,), jnp.int32),
        ]
        + common_scratch(),
        name="second_step",
    )(cover_start, new_tiles, wl, wh, gl, gh, cst, *got, incidence, rl, ra)
    final = jnp.sum(lax.all_to_all(sends, "gx", 0, 0, tiled=True), 0)
    new_vel = final[3:6, None, :NV]
    new_pos = final[0:3, None, :NV] + DT * new_vel
    out = jnp.transpose(last_tiles, (2, 0, 1, 3))
    return out[0:3], out[3:6], new_pos, new_vel


def solution(mesh):
    in_specs = (
        P(None, "wa", "gx", None),
        P(None, "wa", "gx", None),
        P(None, "wa", "gx", None),
        P(None, ("wa", "gx"), None),
        P(None, ("wa", "gx"), None),
        P("wa"),
        P(),
        P(),
        P(),
        P(),
    )
    out_specs = (
        P(None, "wa", "gx", None),
        P(None, "wa", "gx", None),
        P(None, ("wa", "gx"), None),
        P(None, ("wa", "gx"), None),
    )
    return jax.shard_map(body, mesh=mesh, in_specs=in_specs, out_specs=out_specs, check_vma=False)
```

```python
import jax
import jax.numpy as jnp
from jax import lax
from jax.experimental import pallas as pl
from jax.experimental.pallas import tpu as pltpu
from jax.sharding import PartitionSpec as P

SPAN = 3
MAXCOV = 5
DT = 0.04
FAR = 1000.0
ZMID = 16.0
NOISE = 15.0 * 0.7071067811865476
TW = 2
TF = 4
LANES = 128
NV = 498
NVP = 512
NB = 1488
NBP = 1536
NT = 992
NTP = 1024
COLS = NBP + 2 * NTP
SLABS = 32
ROWS = 16

F32 = jnp.float32
BF16 = jnp.bfloat16


def nn(a, b):
    return lax.dot_general(a, b, (((1,), (0,)), ((), ())), preferred_element_type=F32)


def nt(a, b):
    return lax.dot_general(a, b, (((1,), (1,)), ((), ())), preferred_element_type=F32)


def split3(x):
    a = x.astype(BF16).astype(F32)
    r = x - a
    b = r.astype(BF16).astype(F32)
    return a, b, r - b


def row_ids(n):
    return lax.broadcasted_iota(jnp.int32, (8, n), 0)


def rows_of(pieces, n):
    row = row_ids(n)
    out = jnp.zeros((8, n), F32)
    for r, piece in pieces:
        out = jnp.where(row == r, piece, out)
    return out


def dots(st, n):
    row = row_ids(n)
    vel = pltpu.roll(st, 5, 0)
    sq = jnp.sum(jnp.where(row < 3, st * st, 0.0), 0, keepdims=True)
    xv = jnp.sum(jnp.where(row < 3, st * vel, 0.0), 0, keepdims=True)
    return vel, sq, xv


def left_features(st):
    n = st.shape[1]
    a, b, c = split3(st)
    _, sq, xv = dots(st, n)
    s1, s2, s3 = split3(1.0 - sq)
    v1, v2, v3 = split3(xv)
    e1 = rows_of([(0, s1), (1, s2), (2, s3), (3, v1), (4, v2), (5, v3), (6, 1.0), (7, 1.0)], n)
    e2 = rows_of([(0, 1.0)], n)
    return jnp.concatenate([a, a, a, b, b, c, e1, e2], 0)


def right_features(st):
    n = st.shape[1]
    row = row_ids(n)
    vel, sq, xv = dots(st, n)
    s1, s2, s3 = split3(-sq)
    v1, v2, v3 = split3(4.5 * xv)

    def pack(block, e1, e2):
        a, b, c = split3(block)
        return jnp.concatenate([a, b, c, a, b, a, e1, e2], 0).astype(BF16)

    zero = jnp.zeros((8, n), F32)
    near = pack(
        jnp.where(row < 3, 2.0 * st, 0.0),
        rows_of([(0, 1.0), (1, 1.0), (2, 1.0), (6, s1), (7, s2)], n),
        rows_of([(0, s3)], n),
    )
    pos = pltpu.roll(st, 3, 0)
    drag = pack(
        -4.5 * jnp.where(row < 3, vel, jnp.where(row < 6, pos, 0.0)),
        rows_of([(3, 4.5), (4, 4.5), (5, 4.5), (6, v1), (7, v2)], n),
        rows_of([(0, v3)], n),
    )
    up = pltpu.roll(st, 7, 0)
    down = pltpu.roll(st, 1, 0)
    kick = pack(
        NOISE * jnp.where(row == 6, up, jnp.where(row == 7, down, 0.0)),
        rows_of([(6, 25.0)], n),
        zero,
    )
    return near, drag, kick


def sum_features(st):
    n = st.shape[1]
    row = row_ids(n)
    q = jnp.where(row < 3, st, jnp.where(row == 3, 1.0, 0.0))
    a, b, c = split3(q)
    return jnp.concatenate([a, b, c, jnp.zeros((8, n), F32)], 0).astype(BF16)


def halves(s):
    hi = s.astype(BF16)
    return hi, (s - hi.astype(F32)).astype(BF16)


def moment(acc):
    return acc[0:8] + acc[8:16] + acc[16:24]


def cover_slots(starts, j, idx, slot_map, count_ref):
    for m in range(8):
        idx[m] = 0
    count = jnp.int32(0)
    shifts = (-2, -1, 1, 2)
    counts = [jnp.int32(0) for _ in shifts]
    for c in range(SLABS):
        s = starts[c]
        idx[jnp.minimum(count, 7)] = c
        covered = (s <= j) & (j < s + SPAN)
        count = count + covered.astype(jnp.int32)
        if slot_map is not None:
            for k, shift in enumerate(shifts):
                slot_map[k * SLABS + c] = jnp.minimum(counts[k], 7)
                cov = (s <= j + shift) & (j + shift < s + SPAN)
                counts[k] = counts[k] + cov.astype(jnp.int32)
    count = jnp.minimum(count, MAXCOV)
    count_ref[0] = count
    return count


def bond_force(pos, m_ref, par):
    p3 = jnp.concatenate(split3(pos), 0).astype(BF16)

    def fold(x):
        return x[0:24] + x[24:48] + x[48:72]

    def back(g, cols):
        g3 = jnp.concatenate(split3(g), 0).astype(BF16)
        return fold(nt(g3, m_ref[:, cols]))

    one, two, three = slice(0, NBP), slice(NBP, NBP + NTP), slice(NBP + NTP, COLS)
    d = fold(nn(p3, m_ref[:, one]))
    stretch = d[0:8] * d[0:8] + d[8:16] * d[8:16] + d[16:24] * d[16:24]
    coef = (stretch - par[0:1, :]) * par[1:2, :]
    force = back(jnp.concatenate([coef * d[0:8], coef * d[8:16], coef * d[16:24]], 0), one)
    e1 = fold(nn(p3, m_ref[:, two]))
    e2 = fold(nn(p3, m_ref[:, three]))

    def cross(a, b):
        ax, ay, az = a
        bx, by, bz = b
        return ay * bz - az * by, az * bx - ax * bz, ax * by - ay * bx

    a = (e1[0:8], e1[8:16], e1[16:24])
    b = (e2[0:8], e2[8:16], e2[16:24])
    n = cross(a, b)
    area = 0.25 * (n[0] * n[0] + n[1] * n[1] + n[2] * n[2])
    coef = (area - par[2:3, :NTP]) * par[3:4, :NTP]
    g = (coef * n[0], coef * n[1], coef * n[2])
    force = force + back(jnp.concatenate(cross(b, g), 0), two)
    return force + back(jnp.concatenate(cross(g, a), 0), three)


def solvent(near, lfeat, fpart):
    nst = jnp.concatenate(near, 1)
    own = own_of(near)
    ra, rc, rb = right_features(own)
    lfeat[...] = left_features(nst).T.astype(BF16)
    qnear = sum_features(nst)
    for w in range(TW):
        for f in range(TF):
            t = w * TF + f
            cols = slice(t * LANES, (t + 1) * LANES)
            rt = jnp.concatenate([ra[:, cols], rc[:, cols], rb[:, cols]], 1)
            acc = jnp.zeros((32, LANES), F32)
            for dw in range(3):
                first = ((w + dw) * (TF + 2) + f) * LANES
                out = nn(lfeat[first : first + 3 * LANES, :], rt)
                weight = jnp.maximum(out[:, :LANES], 0.0)
                s = weight * (out[:, 2 * LANES :] - weight * out[:, LANES : 2 * LANES])
                hi, lo = halves(s)
                q = qnear[:, first : first + 3 * LANES]
                acc = acc + nn(q, hi) + nn(q, lo)
            fpart[:, cols] = acc
    return own


def own_of(near):
    return jnp.concatenate(
        [near[(w + 1) * (TF + 2) + f + 1] for w in range(TW) for f in range(TF)], 1
    )


def membrane(own, count, cs, lcell, rnear, rdrag, qown, fpart, fcell):
    ra, rc, _ = right_features(own)
    rnear[...] = ra
    rdrag[...] = rc
    qown[...] = sum_features(own)
    fpart[...] = jnp.zeros(fpart.shape, F32)
    fcell[...] = jnp.zeros(fcell.shape, F32)

    def one_cell(m, carry):
        st = cs[m]
        lcell[...] = left_features(st).T.astype(BF16)
        q = sum_features(st)
        total = jnp.zeros((32, NVP), F32)
        for k in range(4):
            cols = slice(k * 256, (k + 1) * 256)
            weight = jnp.maximum(nn(lcell[...], rnear[:, cols]), 0.0)
            s = weight * (4.0 - weight * nn(lcell[...], rdrag[:, cols]))
            hi, lo = halves(s)
            fpart[:, cols] += nn(q, hi) + nn(q, lo)
            qo = qown[:, cols]
            total = total + nt(qo, hi) + nt(qo, lo)
        fcell[m] = total
        return carry

    lax.fori_loop(0, count, one_cell, 0)


def force_of(own, fpart):
    mom = moment(fpart[...])
    return jnp.where(row_ids(own.shape[1]) < 3, own * mom[3:4] - mom, 0.0)


def moved(tile, force):
    st = tile + pltpu.roll(DT * force, 3, 0)
    vel = pltpu.roll(st, 5, 0)
    return st + jnp.where(row_ids(LANES) < 3, DT * vel, 0.0)


def own_frame(t0, t1):
    row = row_ids(LANES)
    out = []
    for w, ref in enumerate((t0, t1)):
        for f in range(TF):
            shift = jnp.where(row == 0, float(w), jnp.where(row == 1, float(f), 0.0))
            out.append(ref[0, f] + jnp.where(row == 2, -ZMID, shift))
    return jnp.concatenate(out, 1)


def near_frames(t0, t1, wl, wh, gl, gh):
    i = lax.axis_index("wa")
    j = lax.axis_index("gx")
    row = row_ids(LANES)
    wlo = jnp.where(i == 0, FAR, 0.0)
    whi = jnp.where(i == ROWS - 1, FAR, 0.0)
    flo = jnp.where(j == 0, FAR, 0.0)
    fhi = jnp.where(j == SLABS - 1, FAR, 0.0)
    near = []
    for w, ref in enumerate((wl, t0, t1, wh)):
        bad_w = wlo if w == 0 else whi if w == TW + 1 else 0.0
        for f in range(TF + 2):
            if f == 0:
                tile, bad = gl[w], bad_w + flo
            elif f == TF + 1:
                tile, bad = gh[w], bad_w + fhi
            else:
                tile, bad = ref[0, f - 1], bad_w
            shift = jnp.where(row == 2, -ZMID, 0.0)
            shift = jnp.where(row == 0, float(w - 1) + bad, shift)
            near.append(tile + jnp.where(row == 1, float(f - 1), shift))
    return near


def early_kernel(
    t0, t1, wl, wh, gl, gh, bonds, corners, rest_len, rest_area,
    out_f, m_ref, par_ref,
    lfeat, fpart,
):
    def fill(start, ids, hi, lo, size, padded):
        m_ref[:, start + padded - LANES : start + padded] = jnp.zeros((NVP, LANES), BF16)
        for a in range(0, size, 512):
            b = min(a + 512, size)
            vid = lax.broadcasted_iota(jnp.int32, (NVP, b - a), 0)
            plus = (vid == ids[hi : hi + 1, a:b]).astype(F32)
            minus = (vid == ids[lo : lo + 1, a:b]).astype(F32)
            m_ref[:, start + a : start + b] = (plus - minus).astype(BF16)

    fill(0, bonds, 0, 1, NB, NBP)
    fill(NBP, corners, 1, 0, NT, NTP)
    fill(NBP + NTP, corners, 2, 0, NT, NTP)
    par_ref[...] = jnp.ones((4, NBP), F32)
    sq = rest_len[...] * rest_len[...]
    par_ref[0:1, 0:NB] = sq
    par_ref[1:2, 0:NB] = -2.0 / sq
    sq = rest_area[...] * rest_area[...]
    par_ref[2:3, 0:NT] = sq
    par_ref[3:4, 0:NT] = -0.125 / sq
    own = solvent(near_frames(t0, t1, wl, wh, gl, gh), lfeat, fpart)
    out_f[...] = force_of(own, fpart)


def lay_rows(ps, m, st):
    for c in range(6):
        ps[c * 8 + m : c * 8 + m + 1, :] = st[c : c + 1, :]


def first_kernel(
    starts, t0, t1, kicks, cells, solv,
    out_0, out_1, out_c, out_r,
    idx, cnt, cs, lcell, rnear, rdrag, qown, fpart, fcell,
):
    j = lax.axis_index("gx")
    count = cover_slots(starts, j, idx, None, cnt)
    out_c[...] = jnp.zeros((48, NVP), F32)
    row = row_ids(NVP)
    shift = jnp.where(row == 1, -(j * TF).astype(F32), jnp.where(row == 2, -ZMID, 0.0))
    away = jnp.where(row < 3, FAR, 0.0)
    for m in range(MAXCOV):
        cs[m] = jnp.zeros((8, NVP), F32)
        for k in range(4):
            cs[m, 0:6, k * LANES : (k + 1) * LANES] = cells[idx[m], k * 6 : k * 6 + 6, :]
        st = jnp.where(m < count, cs[m] + shift, away)
        cs[m] = st
        lay_rows(out_c, m, st)
    own = own_frame(t0, t1)
    membrane(own, count, cs, lcell, rnear, rdrag, qown, fpart, fcell)
    force = solv[...] + force_of(own, fpart)
    for w, (ref, out) in enumerate(((t0, out_0), (t1, out_1))):
        for f in range(TF):
            t = w * TF + f
            st = moved(ref[0, f], force[:, t * LANES : (t + 1) * LANES])
            out[0, f, 0:6, :] = st[0:6]
            out[0, f, 6:8, :] = kicks[w, f]
    out_r[...] = jnp.zeros((24, NVP), F32)
    for m in range(MAXCOV):
        mom = moment(fcell[m])
        react = DT * (cs[m] * mom[3:4] - mom)
        for c in range(3):
            out_r[c * 8 + m : c * 8 + m + 1, :] = react[c : c + 1, :]


def bond_kernel(cst, m_ref, par_ref, out_b):
    out_b[...] = DT * bond_force(cst[0:24, :], m_ref, par_ref)


def second_kernel(
    starts, t0, t1, cst, share, bond, r0, r1, r2, r3, m_ref, par_ref,
    out_f, out_s,
    idx, cnt, smap, cs, ps, lcell, rnear, rdrag, qown, fpart, fcell,
):
    j = lax.axis_index("gx")
    count = cover_slots(starts, j, idx, smap, cnt)
    ps[0:24, :] = cst[0:24, :]
    ps[24:48, :] = cst[24:48, :] + bond[...] + share[...]
    for m in range(MAXCOV):
        cell = idx[m]
        s = starts[cell]
        for k, (shift, ref) in enumerate(((-2, r0), (-1, r1), (1, r2), (2, r3))):
            slot = smap[k * SLABS + cell]
            there = (m < count) & (s <= j + shift) & (j + shift < s + SPAN)
            for c in range(3):
                at = 24 + c * 8 + m
                got = ref[pl.ds(c * 8 + slot, 1), :]
                ps[at : at + 1, :] += jnp.where(there, got, 0.0)
    ps[0:24, :] += DT * ps[24:48, :]
    for m in range(MAXCOV):
        cs[m] = jnp.zeros((8, NVP), F32)
        for c in range(6):
            cs[m, c : c + 1, :] = ps[c * 8 + m : c * 8 + m + 1, :]
    own = own_frame(t0, t1)
    membrane(own, count, cs, lcell, rnear, rdrag, qown, fpart, fcell)
    out_f[...] = force_of(own, fpart)
    ps[24:48, :] += DT * bond_force(ps[0:24, :], m_ref, par_ref)
    out_s[...] = jnp.zeros(out_s.shape, F32)
    row = row_ids(NVP)
    shift = jnp.where(row == 1, (j * TF).astype(F32), jnp.where(row == 2, ZMID, 0.0))
    for m in range(MAXCOV):
        cell = idx[m]
        mom = moment(fcell[m])
        react = DT * (cs[m] * mom[3:4] - mom)
        push = pltpu.roll(jnp.where(row < 3, react, 0.0), 3, 0)
        for c in range(6):
            cs[m, c : c + 1, :] = ps[c * 8 + m : c * 8 + m + 1, :]
        whole = push + jnp.where(starts[cell] == j, cs[m] + shift, 0.0)

        @pl.when(m < count)
        def _():
            for k in range(4):
                out_s[cell, k * 6 : k * 6 + 6, :] = whole[0:6, k * LANES : (k + 1) * LANES]


def late_kernel(t0, t1, wl, wh, gl, gh, memb, out_p, out_v, lfeat, fpart):
    own = solvent(near_frames(t0, t1, wl, wh, gl, gh), lfeat, fpart)
    force = memb[...] + force_of(own, fpart)
    for w, ref in enumerate((t0, t1)):
        for f in range(TF):
            t = w * TF + f
            st = moved(ref[0, f], force[:, t * LANES : (t + 1) * LANES])
            for c in range(3):
                out_p[c, w, f : f + 1, :] = st[c : c + 1]
                out_v[c, w, f : f + 1, :] = st[c + 3 : c + 4]


def vmem():
    return pl.BlockSpec(memory_space=pltpu.VMEM)


def smem():
    return pl.BlockSpec(memory_space=pltpu.SMEM)


def slot_scratch(extra):
    return (
        [pltpu.SMEM((8,), jnp.int32), pltpu.SMEM((1,), jnp.int32)]
        + extra
        + [
            pltpu.VMEM((NVP, 64), BF16),
            pltpu.VMEM((64, 8 * LANES), BF16),
            pltpu.VMEM((64, 8 * LANES), BF16),
            pltpu.VMEM((32, 8 * LANES), BF16),
            pltpu.VMEM((32, 8 * LANES), F32),
            pltpu.VMEM((8, 32, NVP), F32),
        ]
    )


def solvent_scratch():
    return [pltpu.VMEM((24 * LANES, 64), BF16), pltpu.VMEM((32, 8 * LANES), F32)]


def call(kernel, name, outs, scratch, args, scalars=0):
    return pl.pallas_call(
        kernel,
        out_shape=tuple(jax.ShapeDtypeStruct(s, t) for s, t in outs),
        in_specs=[smem()] * scalars + [vmem()] * (len(args) - scalars),
        out_specs=tuple(vmem() for _ in outs),
        scratch_shapes=scratch,
        name=name,
    )(*args)


def moves(axis, shift):
    count = lax.axis_size(axis)
    return [(k, k + shift) for k in range(count) if 0 <= k + shift < count]


def halo(t0, t1):
    wl = lax.ppermute(t1, "wa", moves("wa", 1))
    wh = lax.ppermute(t0, "wa", moves("wa", -1))

    def column(f):
        return jnp.concatenate([wl[:, f], t0[:, f], t1[:, f], wh[:, f]], 0)

    gl = lax.ppermute(column(TF - 1), "gx", moves("gx", 1))
    gh = lax.ppermute(column(0), "gx", moves("gx", -1))
    return wl, wh, gl, gh


def body(
    part_pos, part_vel, random_kicks, vert_pos, vert_vel,
    cover_start, bond_ends, triangles, rest_len, rest_area,
):
    cell = jnp.concatenate(
        [
            jnp.pad(vert_pos[:, 0], ((0, 0), (0, NVP - NV)), constant_values=FAR),
            jnp.pad(vert_vel[:, 0], ((0, 0), (0, NVP - NV))),
        ],
        0,
    )
    cell = jnp.transpose(cell.reshape(6, 4, LANES), (1, 0, 2)).reshape(24, LANES)
    cells = lax.all_to_all(
        jnp.broadcast_to(cell[None], (SLABS, 24, LANES)), "gx", 0, 0, tiled=True
    )
    tiles = jnp.transpose(
        jnp.concatenate([part_pos, part_vel, random_kicks[0:2]], 0), (1, 2, 0, 3)
    )
    t0, t1 = tiles[:1], tiles[1:]
    kicks = jnp.transpose(random_kicks[2:4], (1, 2, 0, 3))
    part = ((8, TW * TF * LANES), F32)
    row = ((1, TF, 8, LANES), F32)
    solv, incidence, par = call(
        early_kernel,
        "early",
        [part, ((NVP, COLS), BF16), ((4, NBP), F32)],
        solvent_scratch(),
        (t0, t1, *halo(t0, t1), bond_ends.T, triangles.T, rest_len[None], rest_area[None]),
    )
    cell_scratch = pltpu.VMEM((8, 8, NVP), F32)
    n0, n1, cst, share = call(
        first_kernel,
        "first",
        [row, row, ((48, NVP), F32), ((24, NVP), F32)],
        slot_scratch([cell_scratch]),
        (cover_start, t0, t1, kicks, cells, solv),
        1,
    )
    got = [lax.ppermute(share, "gx", moves("gx", -s)) for s in (-2, -1, 1, 2)]
    (bond,) = call(bond_kernel, "bond", [((24, NVP), F32)], [], (cst, incidence, par))
    memb, sends = call(
        second_kernel,
        "second",
        [part, ((SLABS, 24, LANES), F32)],
        slot_scratch(
            [pltpu.SMEM((4 * SLABS,), jnp.int32), cell_scratch, pltpu.VMEM((48, NVP), F32)]
        ),
        (cover_start, n0, n1, cst, share, bond, *got, incidence, par),
        1,
    )
    final = jnp.sum(lax.all_to_all(sends, "gx", 0, 0, tiled=True), 0)
    out_pos, out_vel = call(
        late_kernel,
        "late",
        [((3, TW, TF, LANES), F32)] * 2,
        solvent_scratch(),
        (n0, n1, *halo(n0, n1), memb),
    )
    final = jnp.transpose(final.reshape(4, 6, LANES), (1, 0, 2)).reshape(6, NVP)
    new_vel = final[3:6, None, :NV]
    new_pos = final[0:3, None, :NV] + DT * new_vel
    return out_pos, out_vel, new_pos, new_vel


def solution(mesh):
    in_specs = (
        P(None, "wa", "gx", None),
        P(None, "wa", "gx", None),
        P(None, "wa", "gx", None),
        P(None, ("wa", "gx"), None),
        P(None, ("wa", "gx"), None),
        P("wa"),
        P(),
        P(),
        P(),
        P(),
    )
    out_specs = (
        P(None, "wa", "gx", None),
        P(None, "wa", "gx", None),
        P(None, ("wa", "gx"), None),
        P(None, ("wa", "gx"), None),
    )
    return jax.shard_map(body, mesh=mesh, in_specs=in_specs, out_specs=out_specs, check_vma=False)
```

```python
import jax
import jax.numpy as jnp
from jax import lax
from jax.experimental import pallas as pl
from jax.experimental.pallas import tpu as pltpu
from jax.sharding import PartitionSpec as P

SPAN = 3
MAXCOV = 5
DT = 0.04
FAR = 1000.0
ZMID = 16.0
NOISE = 15.0 * 0.7071067811865476
TW = 2
TF = 4
LANES = 128
NV = 498
NVP = 512
NB = 1488
NBP = 1536
NT = 992
NTP = 1024
COLS = NBP + 2 * NTP
SLABS = 32
WIDTH = 2
ROWS = 16

F32 = jnp.float32
BF16 = jnp.bfloat16


def nn(a, b):
    return lax.dot_general(a, b, (((1,), (0,)), ((), ())), preferred_element_type=F32)


def nt(a, b):
    return lax.dot_general(a, b, (((1,), (1,)), ((), ())), preferred_element_type=F32)


def split3(x):
    a = x.astype(BF16).astype(F32)
    r = x - a
    b = r.astype(BF16).astype(F32)
    return a, b, r - b


def row_ids(n):
    return lax.broadcasted_iota(jnp.int32, (8, n), 0)


def rows_of(pieces, n):
    row = row_ids(n)
    out = jnp.zeros((8, n), F32)
    for r, piece in pieces:
        out = jnp.where(row == r, piece, out)
    return out


def dots(st, n):
    row = row_ids(n)
    vel = pltpu.roll(st, 5, 0)
    sq = jnp.sum(jnp.where(row < 3, st * st, 0.0), 0, keepdims=True)
    xv = jnp.sum(jnp.where(row < 3, st * vel, 0.0), 0, keepdims=True)
    return vel, sq, xv


def left_features(st):
    n = st.shape[1]
    a, b, c = split3(st)
    _, sq, xv = dots(st, n)
    s1, s2, s3 = split3(1.0 - sq)
    v1, v2, v3 = split3(xv)
    e1 = rows_of([(0, s1), (1, s2), (2, s3), (3, v1), (4, v2), (5, v3), (6, 1.0), (7, 1.0)], n)
    e2 = rows_of([(0, 1.0)], n)
    return jnp.concatenate([a, a, a, b, b, c, e1, e2], 0)


def right_features(st):
    n = st.shape[1]
    row = row_ids(n)
    vel, sq, xv = dots(st, n)
    s1, s2, s3 = split3(-sq)
    v1, v2, v3 = split3(4.5 * xv)

    def pack(block, e1, e2):
        a, b, c = split3(block)
        return jnp.concatenate([a, b, c, a, b, a, e1, e2], 0).astype(BF16)

    zero = jnp.zeros((8, n), F32)
    near = pack(
        jnp.where(row < 3, 2.0 * st, 0.0),
        rows_of([(0, 1.0), (1, 1.0), (2, 1.0), (6, s1), (7, s2)], n),
        rows_of([(0, s3)], n),
    )
    pos = pltpu.roll(st, 3, 0)
    drag = pack(
        -4.5 * jnp.where(row < 3, vel, jnp.where(row < 6, pos, 0.0)),
        rows_of([(3, 4.5), (4, 4.5), (5, 4.5), (6, v1), (7, v2)], n),
        rows_of([(0, v3)], n),
    )
    up = pltpu.roll(st, 7, 0)
    down = pltpu.roll(st, 1, 0)
    kick = pack(
        NOISE * jnp.where(row == 6, up, jnp.where(row == 7, down, 0.0)),
        rows_of([(6, 25.0)], n),
        zero,
    )
    return near, drag, kick


def sum_features(st):
    n = st.shape[1]
    row = row_ids(n)
    q = jnp.where(row < 3, st, jnp.where(row == 3, 1.0, 0.0))
    a, b, c = split3(q)
    return jnp.concatenate([a, b, c, jnp.zeros((8, n), F32)], 0).astype(BF16)


def halves(s):
    hi = s.astype(BF16)
    return hi, (s - hi.astype(F32)).astype(BF16)


def moment(acc):
    return acc[0:8] + acc[8:16] + acc[16:24]


def cover_slots(starts, j, idx, slot_map, count_ref):
    for m in range(8):
        idx[m] = 0
    count = jnp.int32(0)
    shifts = (-2, -1, 1, 2)
    counts = [jnp.int32(0) for _ in shifts]
    for c in range(SLABS):
        s = starts[c]
        idx[jnp.minimum(count, 7)] = c
        covered = (s <= j) & (j < s + SPAN)
        count = count + covered.astype(jnp.int32)
        if slot_map is not None:
            for k, shift in enumerate(shifts):
                slot_map[k * SLABS + c] = jnp.minimum(counts[k], 7)
                cov = (s <= j + shift) & (j + shift < s + SPAN)
                counts[k] = counts[k] + cov.astype(jnp.int32)
    count = jnp.minimum(count, MAXCOV)
    count_ref[0] = count
    return count


def bond_force(pos, m_ref, par):
    p3 = jnp.concatenate(split3(pos), 0).astype(BF16)

    def fold(x):
        return x[0:24] + x[24:48] + x[48:72]

    def back(g, cols):
        g3 = jnp.concatenate(split3(g), 0).astype(BF16)
        return fold(nt(g3, m_ref[:, cols]))

    one, two, three = slice(0, NBP), slice(NBP, NBP + NTP), slice(NBP + NTP, COLS)
    d = fold(nn(p3, m_ref[:, one]))
    stretch = d[0:8] * d[0:8] + d[8:16] * d[8:16] + d[16:24] * d[16:24]
    coef = (stretch - par[0:1, :]) * par[1:2, :]
    force = back(jnp.concatenate([coef * d[0:8], coef * d[8:16], coef * d[16:24]], 0), one)
    e1 = fold(nn(p3, m_ref[:, two]))
    e2 = fold(nn(p3, m_ref[:, three]))

    def cross(a, b):
        ax, ay, az = a
        bx, by, bz = b
        return ay * bz - az * by, az * bx - ax * bz, ax * by - ay * bx

    a = (e1[0:8], e1[8:16], e1[16:24])
    b = (e2[0:8], e2[8:16], e2[16:24])
    n = cross(a, b)
    area = 0.25 * (n[0] * n[0] + n[1] * n[1] + n[2] * n[2])
    coef = (area - par[2:3, :NTP]) * par[3:4, :NTP]
    g = (coef * n[0], coef * n[1], coef * n[2])
    force = force + back(jnp.concatenate(cross(b, g), 0), two)
    return force + back(jnp.concatenate(cross(g, a), 0), three)


def solvent(near, lfeat, fpart):
    nst = jnp.concatenate(near, 1)
    own = own_of(near)
    ra, rc, rb = right_features(own)
    lfeat[...] = left_features(nst).T.astype(BF16)
    qnear = sum_features(nst)
    for w in range(TW):
        for f in range(TF):
            t = w * TF + f
            cols = slice(t * LANES, (t + 1) * LANES)
            rt = jnp.concatenate([ra[:, cols], rc[:, cols], rb[:, cols]], 1)
            acc = jnp.zeros((32, LANES), F32)
            for dw in range(3):
                first = ((w + dw) * (TF + 2) + f) * LANES
                out = nn(lfeat[first : first + 3 * LANES, :], rt)
                weight = jnp.maximum(out[:, :LANES], 0.0)
                s = weight * (out[:, 2 * LANES :] - weight * out[:, LANES : 2 * LANES])
                hi, lo = halves(s)
                q = qnear[:, first : first + 3 * LANES]
                acc = acc + nn(q, hi) + nn(q, lo)
            fpart[:, cols] = acc
    return own


def own_of(near):
    return jnp.concatenate(
        [near[(w + 1) * (TF + 2) + f + 1] for w in range(TW) for f in range(TF)], 1
    )


def sort_half(st, hot):
    n = st.shape[1]
    z = st[2:3, :]
    column = jnp.broadcast_to(z, (8, n)).T[:, 0:1]
    ranks = []
    for k in range(n // LANES):
        cols = slice(k * LANES, (k + 1) * LANES)
        zj = z[:, cols]
        count = jnp.zeros((1, LANES), F32)
        for b in range(n // LANES):
            zi = column[b * LANES : (b + 1) * LANES]
            if b < k:
                less = zi <= zj
            elif b > k:
                less = zi < zj
            else:
                first = lax.broadcasted_iota(jnp.int32, (LANES, LANES), 0)
                second = lax.broadcasted_iota(jnp.int32, (LANES, LANES), 1)
                less = (zi < zj) | ((zi == zj) & (first < second))
            count = count + jnp.sum(jnp.where(less, 1.0, 0.0), 0, keepdims=True)
        ranks.append(count)
    rank = jnp.concatenate(ranks, 1).astype(jnp.int32)
    place = lax.broadcasted_iota(jnp.int32, (n, n), 0)
    hot[...] = jnp.where(place == rank, 1.0, 0.0).astype(BF16)
    parts = nt(jnp.concatenate(split3(st), 0).astype(BF16), hot[...])
    return parts[0:8] + parts[8:16] + parts[16:24]


def unsort_half(force, hot):
    parts = nn(jnp.concatenate(split3(force), 0).astype(BF16), hot[...])
    return parts[0:8] + parts[8:16] + parts[16:24]


def membrane(own, count, cs, work, hot, lcell, qcell, right, qown, fpart, fcell):
    order = [[w * TF + f for w in range(TW) for f in (2 * g, 2 * g + 1)] for g in range(2)]
    halves_of = [
        sort_half(jnp.concatenate([own[:, t * LANES : (t + 1) * LANES] for t in o], 1), hot.at[g])
        for g, o in enumerate(order)
    ]
    st = jnp.concatenate(halves_of, 1)
    ra, rc, _ = right_features(st)
    q = sum_features(st)
    lane = lax.broadcasted_iota(jnp.int32, (8, LANES), 1)
    low = jnp.full((8, LANES), 3.0e4, F32)
    high = -low
    for k in range(8):
        cols = slice(k * LANES, (k + 1) * LANES)
        right[k] = jnp.concatenate([ra[:, cols], rc[:, cols]], 1)
        qown[k] = jnp.concatenate([q[:, cols], q[:, cols]], 1)
        block = st[:, cols]
        low = jnp.where(lane == k, jnp.min(block, 1, keepdims=True), low)
        high = jnp.where(lane == k, jnp.max(block, 1, keepdims=True), high)
    row = row_ids(LANES)
    bits = jnp.zeros((8, LANES), F32)
    for k in range(8):
        bits = jnp.where(lane == k, float(1 << k), bits)
    real = lax.broadcasted_iota(jnp.int32, (8, NVP), 1) < NV
    right[8] = jnp.zeros((64, 2 * LANES), BF16)
    qown[8] = jnp.zeros((32, 2 * LANES), BF16)
    n = jnp.int32(0)
    for m in range(MAXCOV):
        cell = cs[m]
        cell_low = jnp.min(jnp.where(real, cell, 3.0e4), 1, keepdims=True)
        cell_high = jnp.max(jnp.where(real, cell, -3.0e4), 1, keepdims=True)
        apart = (low - 1.01 > cell_high) | (high + 1.01 < cell_low)
        apart = jnp.max(jnp.where((row < 3) & apart, 1.0, 0.0), 0, keepdims=True)
        mask = jnp.sum(jnp.where(apart > 0.5, 0.0, bits[0:1])).astype(jnp.int32)
        mask = jnp.where(m < count, mask, 0)
        for k in range(8):
            work[n] = m * 16 + k
            n = n + ((mask >> k) & 1)
    for k in range(WIDTH):
        work[n + k] = 8
    fpart[...] = jnp.zeros(fpart.shape, F32)
    fcell[...] = jnp.zeros(fcell.shape, F32)

    def one_cell(m, carry):
        lcell[m] = left_features(cs[m]).T.astype(BF16)
        qcell[m] = sum_features(cs[m])
        return carry

    lax.fori_loop(0, count, one_cell, 0)

    def some_blocks(i, carry):
        found = []
        for u in range(WIDTH):
            item = work[i * WIDTH + u]
            m, k = item >> 4, item & 15
            out = nn(lcell[m], right[k])
            weight = jnp.maximum(out[:, :LANES], 0.0)
            s = weight * (4.0 - weight * out[:, LANES:])
            both = jnp.concatenate(halves(s), 1)
            found.append((m, k, nn(qcell[m], both), nt(qown[k], both)))
        for m, k, on_parts, on_cell in found:
            fpart[k] += on_parts[:, :LANES] + on_parts[:, LANES:]
            fcell[m] += on_cell
        return carry

    lax.fori_loop(0, (n + WIDTH - 1) // WIDTH, some_blocks, 0)
    force = []
    for k in range(8):
        mom = moment(fpart[k])
        block = st[:, k * LANES : (k + 1) * LANES]
        force.append(jnp.where(row < 3, block * mom[3:4] - mom, 0.0))
    tiles = [None] * 8
    for g, o in enumerate(order):
        whole = unsort_half(jnp.concatenate(force[4 * g : 4 * g + 4], 1), hot.at[g])
        for place, t in enumerate(o):
            tiles[t] = whole[:, place * LANES : (place + 1) * LANES]
    return jnp.concatenate(tiles, 1)


def force_of(own, fpart):
    mom = moment(fpart[...])
    return jnp.where(row_ids(own.shape[1]) < 3, own * mom[3:4] - mom, 0.0)


def moved(tile, force):
    st = tile + pltpu.roll(DT * force, 3, 0)
    vel = pltpu.roll(st, 5, 0)
    return st + jnp.where(row_ids(LANES) < 3, DT * vel, 0.0)


def own_frame(t0, t1):
    row = row_ids(LANES)
    out = []
    for w, ref in enumerate((t0, t1)):
        for f in range(TF):
            shift = jnp.where(row == 0, float(w), jnp.where(row == 1, float(f), 0.0))
            out.append(ref[0, f] + jnp.where(row == 2, -ZMID, shift))
    return jnp.concatenate(out, 1)


def near_frames(t0, t1, in_a, in_b, gl, gh):
    i = lax.axis_index("wa")
    j = lax.axis_index("gx")
    row = row_ids(LANES)
    wlo = jnp.where(i == 0, FAR, 0.0)
    whi = jnp.where(i == ROWS - 1, FAR, 0.0)
    flo = jnp.where(j == 0, FAR, 0.0)
    fhi = jnp.where(j == SLABS - 1, FAR, 0.0)
    near = []
    even = i % 2 == 0
    for w, ref in enumerate((None, t0, t1, None)):
        bad_w = wlo if w == 0 else whi if w == TW + 1 else 0.0
        for f in range(TF + 2):
            if f == 0:
                tile, bad = gl[w], bad_w + flo
            elif f == TF + 1:
                tile, bad = gh[w], bad_w + fhi
            else:
                a, b = (in_b, in_a) if w == 0 else (in_a, in_b)
                tile = jnp.where(even, a[0, f - 1], b[0, f - 1]) if ref is None else ref[0, f - 1]
                bad = bad_w
            shift = jnp.where(row == 2, -ZMID, 0.0)
            shift = jnp.where(row == 0, float(w - 1) + bad, shift)
            near.append(tile + jnp.where(row == 1, float(f - 1), shift))
    return near


def incidence_kernel(bonds, corners, rest_len, rest_area, m_ref, par_ref):
    def fill(start, ids, hi, lo, size, padded):
        m_ref[:, start + padded - LANES : start + padded] = jnp.zeros((NVP, LANES), BF16)
        for a in range(0, size, 512):
            b = min(a + 512, size)
            vid = lax.broadcasted_iota(jnp.int32, (NVP, b - a), 0)
            plus = (vid == ids[hi : hi + 1, a:b]).astype(F32)
            minus = (vid == ids[lo : lo + 1, a:b]).astype(F32)
            m_ref[:, start + a : start + b] = (plus - minus).astype(BF16)

    fill(0, bonds, 0, 1, NB, NBP)
    fill(NBP, corners, 1, 0, NT, NTP)
    fill(NBP + NTP, corners, 2, 0, NT, NTP)
    par_ref[...] = jnp.ones((4, NBP), F32)
    sq = rest_len[...] * rest_len[...]
    par_ref[0:1, 0:NB] = sq
    par_ref[1:2, 0:NB] = -2.0 / sq
    sq = rest_area[...] * rest_area[...]
    par_ref[2:3, 0:NT] = sq
    par_ref[3:4, 0:NT] = -0.125 / sq


def early_kernel(t0, t1, in_a, in_b, gl, gh, out_f, lfeat, fpart):
    own = solvent(near_frames(t0, t1, in_a, in_b, gl, gh), lfeat, fpart)
    out_f[...] = force_of(own, fpart)


def lay_rows(ps, m, st):
    for c in range(6):
        ps[c * 8 + m : c * 8 + m + 1, :] = st[c : c + 1, :]


def first_kernel(
    starts, t0, t1, kicks, cells, solv,
    out_0, out_1, out_a, out_b, out_c, out_r,
    idx, cnt, cs, work, hot, lcell, qcell, right, qown, fpart, fcell,
):
    j = lax.axis_index("gx")
    count = cover_slots(starts, j, idx, None, cnt)
    out_c[...] = jnp.zeros((48, NVP), F32)
    row = row_ids(NVP)
    shift = jnp.where(row == 1, -(j * TF).astype(F32), jnp.where(row == 2, -ZMID, 0.0))
    away = jnp.where(row < 3, FAR, 0.0)
    for m in range(MAXCOV):
        cs[m] = jnp.zeros((8, NVP), F32)
        for k in range(4):
            cs[m, 0:6, k * LANES : (k + 1) * LANES] = cells[idx[m], k * 6 : k * 6 + 6, :]
        st = jnp.where(m < count, cs[m] + shift, away)
        cs[m] = st
        lay_rows(out_c, m, st)
    own = own_frame(t0, t1)
    force = solv[...] + membrane(own, count, cs, work, hot, lcell, qcell, right, qown, fpart, fcell)
    for w, (ref, out) in enumerate(((t0, out_0), (t1, out_1))):
        for f in range(TF):
            t = w * TF + f
            st = moved(ref[0, f], force[:, t * LANES : (t + 1) * LANES])
            out[0, f, 0:6, :] = st[0:6]
            out[0, f, 6:8, :] = kicks[w, f]
    even = lax.axis_index("wa") % 2 == 0
    out_a[...] = jnp.where(even, out_1[...], out_0[...])
    out_b[...] = jnp.where(even, out_0[...], out_1[...])
    out_r[...] = jnp.zeros((24, NVP), F32)
    for m in range(MAXCOV):
        mom = moment(fcell[m])
        react = DT * (cs[m] * mom[3:4] - mom)
        for c in range(3):
            out_r[c * 8 + m : c * 8 + m + 1, :] = react[c : c + 1, :]


def bond_kernel(cst, m_ref, par_ref, out_b):
    out_b[...] = DT * bond_force(cst[0:24, :], m_ref, par_ref)


def second_kernel(
    starts, t0, t1, cst, share, bond, r0, r1, r2, r3, m_ref, par_ref,
    out_f, out_s,
    idx, cnt, smap, cs, ps, work, hot, lcell, qcell, right, qown, fpart, fcell,
):
    j = lax.axis_index("gx")
    count = cover_slots(starts, j, idx, smap, cnt)
    ps[0:24, :] = cst[0:24, :]
    ps[24:48, :] = cst[24:48, :] + bond[...] + share[...]
    for m in range(MAXCOV):
        cell = idx[m]
        s = starts[cell]
        for k, (shift, ref) in enumerate(((-2, r0), (-1, r1), (1, r2), (2, r3))):
            slot = smap[k * SLABS + cell]
            there = (m < count) & (s <= j + shift) & (j + shift < s + SPAN)
            for c in range(3):
                at = 24 + c * 8 + m
                got = ref[pl.ds(c * 8 + slot, 1), :]
                ps[at : at + 1, :] += jnp.where(there, got, 0.0)
    ps[0:24, :] += DT * ps[24:48, :]
    for m in range(MAXCOV):
        cs[m] = jnp.zeros((8, NVP), F32)
        for c in range(6):
            cs[m, c : c + 1, :] = ps[c * 8 + m : c * 8 + m + 1, :]
    own = own_frame(t0, t1)
    out_f[...] = membrane(own, count, cs, work, hot, lcell, qcell, right, qown, fpart, fcell)
    ps[24:48, :] += DT * bond_force(ps[0:24, :], m_ref, par_ref)
    out_s[...] = jnp.zeros(out_s.shape, F32)
    row = row_ids(NVP)
    shift = jnp.where(row == 1, (j * TF).astype(F32), jnp.where(row == 2, ZMID, 0.0))
    for m in range(MAXCOV):
        cell = idx[m]
        mom = moment(fcell[m])
        react = DT * (cs[m] * mom[3:4] - mom)
        push = pltpu.roll(jnp.where(row < 3, react, 0.0), 3, 0)
        for c in range(6):
            cs[m, c : c + 1, :] = ps[c * 8 + m : c * 8 + m + 1, :]
        whole = push + jnp.where(starts[cell] == j, cs[m] + shift, 0.0)

        @pl.when(m < count)
        def _():
            for k in range(4):
                out_s[cell, k * 6 : k * 6 + 6, :] = whole[0:6, k * LANES : (k + 1) * LANES]


def late_kernel(t0, t1, in_a, in_b, gl, gh, memb, out_p, out_v, lfeat, fpart):
    own = solvent(near_frames(t0, t1, in_a, in_b, gl, gh), lfeat, fpart)
    force = memb[...] + force_of(own, fpart)
    for w, ref in enumerate((t0, t1)):
        for f in range(TF):
            t = w * TF + f
            st = moved(ref[0, f], force[:, t * LANES : (t + 1) * LANES])
            for c in range(3):
                out_p[c, w, f : f + 1, :] = st[c : c + 1]
                out_v[c, w, f : f + 1, :] = st[c + 3 : c + 4]


def vmem():
    return pl.BlockSpec(memory_space=pltpu.VMEM)


def smem():
    return pl.BlockSpec(memory_space=pltpu.SMEM)


def slot_scratch(extra):
    return (
        [pltpu.SMEM((8,), jnp.int32), pltpu.SMEM((1,), jnp.int32)]
        + extra
        + [
            pltpu.SMEM((48,), jnp.int32),
            pltpu.VMEM((2, 4 * LANES, 4 * LANES), BF16),
            pltpu.VMEM((MAXCOV, NVP, 64), BF16),
            pltpu.VMEM((MAXCOV, 32, NVP), BF16),
            pltpu.VMEM((9, 64, 2 * LANES), BF16),
            pltpu.VMEM((9, 32, 2 * LANES), BF16),
            pltpu.VMEM((9, 32, LANES), F32),
            pltpu.VMEM((8, 32, NVP), F32),
        ]
    )


def solvent_scratch():
    return [pltpu.VMEM((24 * LANES, 64), BF16), pltpu.VMEM((32, 8 * LANES), F32)]


def call(kernel, name, outs, scratch, args, scalars=0):
    return pl.pallas_call(
        kernel,
        out_shape=tuple(jax.ShapeDtypeStruct(s, t) for s, t in outs),
        in_specs=[smem()] * scalars + [vmem()] * (len(args) - scalars),
        out_specs=tuple(vmem() for _ in outs),
        scratch_shapes=scratch,
        name=name,
    )(*args)


def moves(axis, shift):
    count = lax.axis_size(axis)
    return [(k, k + shift) for k in range(count) if 0 <= k + shift < count]


def swap(out_a, out_b):
    count = lax.axis_size("wa")
    odd_pairs = [(k, k - 1 if k % 2 == 0 else k + 1) for k in range(1, count - 1)]
    in_a = lax.ppermute(out_a, "wa", [(k, k ^ 1) for k in range(count)])
    return in_a, lax.ppermute(out_b, "wa", odd_pairs)


def columns(t0, t1, in_a, in_b):
    even = lax.axis_index("wa") % 2 == 0

    def column(f):
        a, b = in_a[:, f], in_b[:, f]
        return jnp.concatenate(
            [jnp.where(even, b, a), t0[:, f], t1[:, f], jnp.where(even, a, b)], 0
        )

    gl = lax.ppermute(column(TF - 1), "gx", moves("gx", 1))
    gh = lax.ppermute(column(0), "gx", moves("gx", -1))
    return gl, gh


def body(
    part_pos, part_vel, random_kicks, vert_pos, vert_vel,
    cover_start, bond_ends, triangles, rest_len, rest_area,
):
    cell = jnp.concatenate(
        [
            jnp.pad(vert_pos[:, 0], ((0, 0), (0, NVP - NV)), constant_values=FAR),
            jnp.pad(vert_vel[:, 0], ((0, 0), (0, NVP - NV))),
        ],
        0,
    )
    cell = jnp.transpose(cell.reshape(6, 4, LANES), (1, 0, 2)).reshape(24, LANES)
    tiles = jnp.transpose(
        jnp.concatenate([part_pos, part_vel, random_kicks[0:2]], 0), (1, 2, 0, 3)
    )
    t0, t1 = tiles[:1], tiles[1:]
    even = lax.axis_index("wa") % 2 == 0
    kicks = jnp.transpose(random_kicks[2:4], (1, 2, 0, 3))
    part = ((8, TW * TF * LANES), F32)
    row = ((1, TF, 8, LANES), F32)
    incidence, par = call(
        incidence_kernel,
        "incidence",
        [((NVP, COLS), BF16), ((4, NBP), F32)],
        [],
        (bond_ends.T, triangles.T, rest_len[None], rest_area[None]),
    )
    incidence, cell, t0, t1 = lax.optimization_barrier((incidence, cell, t0, t1))
    cells = lax.all_to_all(
        jnp.broadcast_to(cell[None], (SLABS, 24, LANES)), "gx", 0, 0, tiled=True
    )
    sides = (jnp.where(even, t1, t0), jnp.where(even, t0, t1))
    swapped = swap(*sides)
    (solv,) = call(
        early_kernel,
        "early",
        [part],
        solvent_scratch(),
        (t0, t1, *swapped, *columns(t0, t1, *swapped)),
    )
    cell_scratch = pltpu.VMEM((8, 8, NVP), F32)
    n0, n1, n_a, n_b, cst, share = call(
        first_kernel,
        "first",
        [row, row, row, row, ((48, NVP), F32), ((24, NVP), F32)],
        slot_scratch([cell_scratch]),
        (cover_start, t0, t1, kicks, cells, solv),
        1,
    )
    swapped = swap(n_a, n_b)
    got = [lax.ppermute(share, "gx", moves("gx", -s)) for s in (-2, -1, 1, 2)]
    (bond,) = call(bond_kernel, "bond", [((24, NVP), F32)], [], (cst, incidence, par))
    bond, *swapped = lax.optimization_barrier((bond, *swapped))
    memb, sends = call(
        second_kernel,
        "second",
        [part, ((SLABS, 24, LANES), F32)],
        slot_scratch(
            [pltpu.SMEM((4 * SLABS,), jnp.int32), cell_scratch, pltpu.VMEM((48, NVP), F32)]
        ),
        (cover_start, n0, n1, cst, share, bond, *got, incidence, par),
        1,
    )
    final = jnp.sum(lax.all_to_all(sends, "gx", 0, 0, tiled=True), 0)
    out_pos, out_vel = call(
        late_kernel,
        "late",
        [((3, TW, TF, LANES), F32)] * 2,
        solvent_scratch(),
        (n0, n1, *swapped, *columns(n0, n1, *swapped), memb),
    )
    final = jnp.transpose(final.reshape(4, 6, LANES), (1, 0, 2)).reshape(6, NVP)
    new_vel = final[3:6, None, :NV]
    new_pos = final[0:3, None, :NV] + DT * new_vel
    return out_pos, out_vel, new_pos, new_vel


def solution(mesh):
    in_specs = (
        P(None, "wa", "gx", None),
        P(None, "wa", "gx", None),
        P(None, "wa", "gx", None),
        P(None, ("wa", "gx"), None),
        P(None, ("wa", "gx"), None),
        P("wa"),
        P(),
        P(),
        P(),
        P(),
    )
    out_specs = (
        P(None, "wa", "gx", None),
        P(None, "wa", "gx", None),
        P(None, ("wa", "gx"), None),
        P(None, ("wa", "gx"), None),
    )
    return jax.shard_map(body, mesh=mesh, in_specs=in_specs, out_specs=out_specs, check_vma=False)
```

```python
import jax
import jax.numpy as jnp
from jax import lax
from jax.experimental import pallas as pl
from jax.experimental.pallas import tpu as pltpu
from jax.sharding import PartitionSpec as P


SPAN = 3
MAXCOV = 5
DT = 0.04
FAR = 1000.0
ZMID = 16.0
NOISE = 15.0 * 0.7071067811865476
TW = 2
TF = 4
LANES = 128
NV = 498
NVP = 512
NB = 1488
NBP = 512
NT = 992
NTP = 384
COLS = NBP + 2 * NTP
SLABS = 32
WIDTH = 2
ROWS = 16

F32 = jnp.float32
BF16 = jnp.bfloat16


def nn(a, b):
    return lax.dot_general(a, b, (((1,), (0,)), ((), ())), preferred_element_type=F32)


def nt(a, b):
    return lax.dot_general(a, b, (((1,), (1,)), ((), ())), preferred_element_type=F32)


def split3(x):
    a = x.astype(BF16).astype(F32)
    r = x - a
    b = r.astype(BF16).astype(F32)
    return a, b, r - b


def row_ids(n):
    return lax.broadcasted_iota(jnp.int32, (8, n), 0)


def rows_of(pieces, n):
    row = row_ids(n)
    out = jnp.zeros((8, n), F32)
    for r, piece in pieces:
        out = jnp.where(row == r, piece, out)
    return out


def dots(st, n):
    row = row_ids(n)
    vel = pltpu.roll(st, 5, 0)
    sq = jnp.sum(jnp.where(row < 3, st * st, 0.0), 0, keepdims=True)
    xv = jnp.sum(jnp.where(row < 3, st * vel, 0.0), 0, keepdims=True)
    return vel, sq, xv


def left_features(st):
    n = st.shape[1]
    a, b, c = split3(st)
    _, sq, xv = dots(st, n)
    s1, s2, s3 = split3(1.0 - sq)
    v1, v2, v3 = split3(xv)
    e1 = rows_of([(0, s1), (1, s2), (2, s3), (3, v1), (4, v2), (5, v3), (6, 1.0), (7, 1.0)], n)
    e2 = rows_of([(0, 1.0)], n)
    return jnp.concatenate([a, a, a, b, b, c, e1, e2], 0)


def right_features(st):
    n = st.shape[1]
    row = row_ids(n)
    vel, sq, xv = dots(st, n)
    s1, s2, s3 = split3(-sq)
    v1, v2, v3 = split3(4.5 * xv)

    def pack(block, e1, e2):
        a, b, c = split3(block)
        return jnp.concatenate([a, b, c, a, b, a, e1, e2], 0).astype(BF16)

    zero = jnp.zeros((8, n), F32)
    near = pack(
        jnp.where(row < 3, 2.0 * st, 0.0),
        rows_of([(0, 1.0), (1, 1.0), (2, 1.0), (6, s1), (7, s2)], n),
        rows_of([(0, s3)], n),
    )
    pos = pltpu.roll(st, 3, 0)
    drag = pack(
        -4.5 * jnp.where(row < 3, vel, jnp.where(row < 6, pos, 0.0)),
        rows_of([(3, 4.5), (4, 4.5), (5, 4.5), (6, v1), (7, v2)], n),
        rows_of([(0, v3)], n),
    )
    up = pltpu.roll(st, 7, 0)
    down = pltpu.roll(st, 1, 0)
    kick = pack(
        NOISE * jnp.where(row == 6, up, jnp.where(row == 7, down, 0.0)),
        rows_of([(6, 25.0)], n),
        zero,
    )
    return near, drag, kick


def sum_features(st):
    n = st.shape[1]
    row = row_ids(n)
    q = jnp.where(row < 3, st, jnp.where(row == 3, 1.0, 0.0))
    a, b, c = split3(q)
    return jnp.concatenate([a, b, c, jnp.zeros((8, n), F32)], 0).astype(BF16)


def halves(s):
    hi = s.astype(BF16)
    return hi, (s - hi.astype(F32)).astype(BF16)


def moment(acc):
    return acc[0:8] + acc[8:16] + acc[16:24]


def cover_slots(starts, j, idx, slot_map, count_ref):
    for m in range(8):
        idx[m] = 0
    count = jnp.int32(0)
    shifts = (-2, -1, 1, 2)
    counts = [jnp.int32(0) for _ in shifts]
    for c in range(SLABS):
        s = starts[c]
        idx[jnp.minimum(count, 7)] = c
        covered = (s <= j) & (j < s + SPAN)
        count = count + covered.astype(jnp.int32)
        if slot_map is not None:
            for k, shift in enumerate(shifts):
                slot_map[k * SLABS + c] = jnp.minimum(counts[k], 7)
                cov = (s <= j + shift) & (j + shift < s + SPAN)
                counts[k] = counts[k] + cov.astype(jnp.int32)
    count = jnp.minimum(count, MAXCOV)
    count_ref[0] = count
    return count


def bond_force(pos, m_ref, par):
    p3 = jnp.concatenate(split3(pos), 0).astype(BF16)

    def fold(x):
        return x[0:24] + x[24:48] + x[48:72]

    def back(g, cols):
        g3 = jnp.concatenate(split3(g), 0).astype(BF16)
        return fold(nt(g3, m_ref[:, cols]))

    one, two, three = slice(0, NBP), slice(NBP, NBP + NTP), slice(NBP + NTP, COLS)
    d = fold(nn(p3, m_ref[:, one]))
    stretch = d[0:8] * d[0:8] + d[8:16] * d[8:16] + d[16:24] * d[16:24]
    coef = (stretch - par[0:1, :]) * par[1:2, :]
    force = back(jnp.concatenate([coef * d[0:8], coef * d[8:16], coef * d[16:24]], 0), one)
    e1 = fold(nn(p3, m_ref[:, two]))
    e2 = fold(nn(p3, m_ref[:, three]))

    def cross(a, b):
        ax, ay, az = a
        bx, by, bz = b
        return ay * bz - az * by, az * bx - ax * bz, ax * by - ay * bx

    a = (e1[0:8], e1[8:16], e1[16:24])
    b = (e2[0:8], e2[8:16], e2[16:24])
    n = cross(a, b)
    area = 0.25 * (n[0] * n[0] + n[1] * n[1] + n[2] * n[2])
    coef = (area - par[2:3, :NTP]) * par[3:4, :NTP]
    g = (coef * n[0], coef * n[1], coef * n[2])
    force = force + back(jnp.concatenate(cross(b, g), 0), two)
    return force + back(jnp.concatenate(cross(g, a), 0), three)


def solvent(near, lfeat, fpart):
    nst = jnp.concatenate(near, 1)
    own = own_of(near)
    ra, rc, rb = right_features(own)
    lfeat[...] = left_features(nst).T.astype(BF16)
    qnear = sum_features(nst)
    for w in range(TW):
        for f in range(TF):
            t = w * TF + f
            cols = slice(t * LANES, (t + 1) * LANES)
            rt = jnp.concatenate([ra[:, cols], rc[:, cols], rb[:, cols]], 1)
            firsts = [((w + dw) * (TF + 2) + f) * LANES for dw in range(3)]
            near_rows = jnp.concatenate([lfeat[a : a + 3 * LANES, :] for a in firsts], 0)
            out = nn(near_rows, rt)
            weight = jnp.maximum(out[:, :LANES], 0.0)
            s = weight * (out[:, 2 * LANES :] - weight * out[:, LANES : 2 * LANES])
            q = jnp.concatenate([qnear[:, a : a + 3 * LANES] for a in firsts], 1)
            acc = nn(q, jnp.concatenate(halves(s), 1))
            fpart[:, cols] = acc[:, :LANES] + acc[:, LANES:]
    return own


def own_of(near):
    return jnp.concatenate(
        [near[(w + 1) * (TF + 2) + f + 1] for w in range(TW) for f in range(TF)], 1
    )


def sort_half(st, hot):
    n = st.shape[1]
    z = st[2:3, :]
    column = jnp.broadcast_to(z, (8, n)).T[:, 0:1]
    ranks = []
    for k in range(n // LANES):
        cols = slice(k * LANES, (k + 1) * LANES)
        zj = z[:, cols]
        count = jnp.zeros((1, LANES), F32)
        for b in range(n // LANES):
            zi = column[b * LANES : (b + 1) * LANES]
            if b < k:
                less = zi <= zj
            elif b > k:
                less = zi < zj
            else:
                first = lax.broadcasted_iota(jnp.int32, (LANES, LANES), 0)
                second = lax.broadcasted_iota(jnp.int32, (LANES, LANES), 1)
                less = (zi < zj) | ((zi == zj) & (first < second))
            count = count + jnp.sum(jnp.where(less, 1.0, 0.0), 0, keepdims=True)
        ranks.append(count)
    rank = jnp.concatenate(ranks, 1).astype(jnp.int32)
    place = lax.broadcasted_iota(jnp.int32, (n, n), 0)
    hot[...] = jnp.where(place == rank, 1.0, 0.0).astype(BF16)
    parts = nt(jnp.concatenate(split3(st), 0).astype(BF16), hot[...])
    return parts[0:8] + parts[8:16] + parts[16:24]


def unsort_half(force, hot):
    parts = nn(jnp.concatenate(split3(force), 0).astype(BF16), hot[...])
    return parts[0:8] + parts[8:16] + parts[16:24]


def membrane(own, count, cs, work, hot, lcell, qcell, right, qown, fpart, fcell):
    order = [[w * TF + f for w in range(TW) for f in (2 * g, 2 * g + 1)] for g in range(2)]
    halves_of = [
        sort_half(jnp.concatenate([own[:, t * LANES : (t + 1) * LANES] for t in o], 1), hot.at[g])
        for g, o in enumerate(order)
    ]
    st = jnp.concatenate(halves_of, 1)
    ra, rc, _ = right_features(st)
    q = sum_features(st)
    lane = lax.broadcasted_iota(jnp.int32, (8, LANES), 1)
    low = jnp.full((8, LANES), 3.0e4, F32)
    high = -low
    for k in range(8):
        cols = slice(k * LANES, (k + 1) * LANES)
        right[k] = jnp.concatenate([ra[:, cols], rc[:, cols]], 1)
        qown[k] = jnp.concatenate([q[:, cols], q[:, cols]], 1)
        block = st[:, cols]
        low = jnp.where(lane == k, jnp.min(block, 1, keepdims=True), low)
        high = jnp.where(lane == k, jnp.max(block, 1, keepdims=True), high)
    row = row_ids(LANES)
    bits = jnp.zeros((8, LANES), F32)
    for k in range(8):
        bits = jnp.where(lane == k, float(1 << k), bits)
    real = lax.broadcasted_iota(jnp.int32, (8, NVP), 1) < NV
    right[8] = jnp.zeros((64, 2 * LANES), BF16)
    qown[8] = jnp.zeros((32, 2 * LANES), BF16)
    n = jnp.int32(0)
    for m in range(MAXCOV):
        cell = cs[m]
        cell_low = jnp.min(jnp.where(real, cell, 3.0e4), 1, keepdims=True)
        cell_high = jnp.max(jnp.where(real, cell, -3.0e4), 1, keepdims=True)
        apart = (low - 1.01 > cell_high) | (high + 1.01 < cell_low)
        apart = jnp.max(jnp.where((row < 3) & apart, 1.0, 0.0), 0, keepdims=True)
        mask = jnp.sum(jnp.where(apart > 0.5, 0.0, bits[0:1])).astype(jnp.int32)
        mask = jnp.where(m < count, mask, 0)
        for k in range(8):
            work[n] = m * 16 + k
            n = n + ((mask >> k) & 1)
    for k in range(WIDTH):
        work[n + k] = 8
    fpart[...] = jnp.zeros(fpart.shape, F32)
    fcell[...] = jnp.zeros(fcell.shape, F32)

    def one_cell(m, carry):
        lcell[m] = left_features(cs[m]).T.astype(BF16)
        qcell[m] = sum_features(cs[m])
        return carry

    lax.fori_loop(0, count, one_cell, 0)

    def some_blocks(i, carry):
        found = []
        for u in range(WIDTH):
            item = work[i * WIDTH + u]
            m, k = item >> 4, item & 15
            out = nn(lcell[m], right[k])
            weight = jnp.maximum(out[:, :LANES], 0.0)
            s = weight * (4.0 - weight * out[:, LANES:])
            both = jnp.concatenate(halves(s), 1)
            found.append((m, k, nn(qcell[m], both), nt(qown[k], both)))
        for m, k, on_parts, on_cell in found:
            fpart[k] += on_parts[:, :LANES] + on_parts[:, LANES:]
            fcell[m] += on_cell
        return carry

    lax.fori_loop(0, (n + WIDTH - 1) // WIDTH, some_blocks, 0)
    force = []
    for k in range(8):
        mom = moment(fpart[k])
        block = st[:, k * LANES : (k + 1) * LANES]
        force.append(jnp.where(row < 3, block * mom[3:4] - mom, 0.0))
    tiles = [None] * 8
    for g, o in enumerate(order):
        whole = unsort_half(jnp.concatenate(force[4 * g : 4 * g + 4], 1), hot.at[g])
        for place, t in enumerate(o):
            tiles[t] = whole[:, place * LANES : (place + 1) * LANES]
    return jnp.concatenate(tiles, 1)


def force_of(own, fpart):
    mom = moment(fpart[...])
    return jnp.where(row_ids(own.shape[1]) < 3, own * mom[3:4] - mom, 0.0)


def moved(tile, force):
    st = tile + pltpu.roll(DT * force, 3, 0)
    vel = pltpu.roll(st, 5, 0)
    return st + jnp.where(row_ids(LANES) < 3, DT * vel, 0.0)


def own_frame(t0, t1):
    row = row_ids(LANES)
    out = []
    for w, ref in enumerate((t0, t1)):
        for f in range(TF):
            shift = jnp.where(row == 0, float(w), jnp.where(row == 1, float(f), 0.0))
            out.append(ref[0, f] + jnp.where(row == 2, -ZMID, shift))
    return jnp.concatenate(out, 1)


def near_frames(t0, t1, in_a, in_b, gl, gh):
    i = lax.axis_index("wa")
    j = lax.axis_index("gx")
    row = row_ids(LANES)
    wlo = jnp.where(i == 0, FAR, 0.0)
    whi = jnp.where(i == ROWS - 1, FAR, 0.0)
    flo = jnp.where(j == 0, FAR, 0.0)
    fhi = jnp.where(j == SLABS - 1, FAR, 0.0)
    near = []
    even = i % 2 == 0
    for w, ref in enumerate((None, t0, t1, None)):
        bad_w = wlo if w == 0 else whi if w == TW + 1 else 0.0
        for f in range(TF + 2):
            if f == 0:
                tile, bad = gl[w], bad_w + flo
            elif f == TF + 1:
                tile, bad = gh[w], bad_w + fhi
            else:
                a, b = (in_b, in_a) if w == 0 else (in_a, in_b)
                tile = jnp.where(even, a[0, f - 1], b[0, f - 1]) if ref is None else ref[0, f - 1]
                bad = bad_w
            shift = jnp.where(row == 2, -ZMID, 0.0)
            shift = jnp.where(row == 0, float(w - 1) + bad, shift)
            near.append(tile + jnp.where(row == 1, float(f - 1), shift))
    return near


def incidence_kernel(ids, rests, m_ref, par_ref):
    third = lax.axis_index("gx") % SPAN
    bonds = pl.ds(pl.multiple_of(third * NBP, LANES), NBP)
    corners = pl.ds(pl.multiple_of(third * NTP, LANES), NTP)
    vid = lax.broadcasted_iota(jnp.int32, (NVP, NBP), 0)

    def column(hi, lo):
        plus = (vid[:, : hi.shape[1]] == hi).astype(F32)
        return (plus - (vid[:, : hi.shape[1]] == lo).astype(F32)).astype(BF16)

    m_ref[:, 0:NBP] = column(ids[0:1, bonds], ids[1:2, bonds])
    m_ref[:, NBP : NBP + NTP] = column(ids[3:4, corners], ids[2:3, corners])
    m_ref[:, NBP + NTP : COLS] = column(ids[4:5, corners], ids[2:3, corners])
    sq = rests[0:1, bonds] * rests[0:1, bonds]
    par_ref[0:1, :] = sq
    par_ref[1:2, :] = -2.0 / sq
    sq = rests[1:2, corners] * rests[1:2, corners]
    par_ref[2:3, 0:NTP] = sq
    par_ref[3:4, 0:NTP] = -0.125 / sq
    par_ref[2:4, NTP:NBP] = jnp.ones((2, NBP - NTP), F32)


def early_kernel(t0, t1, in_a, in_b, gl, gh, out_f, lfeat, fpart):
    own = solvent(near_frames(t0, t1, in_a, in_b, gl, gh), lfeat, fpart)
    out_f[...] = force_of(own, fpart)


def lay_rows(ps, m, st):
    for c in range(6):
        ps[c * 8 + m : c * 8 + m + 1, :] = st[c : c + 1, :]


def first_kernel(
    starts, t0, t1, kicks, cells, solv, m_ref, par_ref,
    out_0, out_1, out_a, out_b, out_c, out_r,
    idx, cnt, cs, work, hot, lcell, qcell, right, qown, fpart, fcell,
):
    j = lax.axis_index("gx")
    count = cover_slots(starts, j, idx, None, cnt)
    out_c[...] = jnp.zeros((48, NVP), F32)
    row = row_ids(NVP)
    shift = jnp.where(row == 1, -(j * TF).astype(F32), jnp.where(row == 2, -ZMID, 0.0))
    away = jnp.where(row < 3, FAR, 0.0)
    for m in range(MAXCOV):
        cs[m] = jnp.zeros((8, NVP), F32)
        for k in range(4):
            cs[m, 0:6, k * LANES : (k + 1) * LANES] = cells[idx[m], k * 6 : k * 6 + 6, :]
        st = jnp.where(m < count, cs[m] + shift, away)
        cs[m] = st
        lay_rows(out_c, m, st)
    own = own_frame(t0, t1)
    force = solv[...] + membrane(own, count, cs, work, hot, lcell, qcell, right, qown, fpart, fcell)
    for w, (ref, out) in enumerate(((t0, out_0), (t1, out_1))):
        for f in range(TF):
            t = w * TF + f
            st = moved(ref[0, f], force[:, t * LANES : (t + 1) * LANES])
            out[0, f, 0:6, :] = st[0:6]
            out[0, f, 6:8, :] = kicks[w, f]
    even = lax.axis_index("wa") % 2 == 0
    out_a[...] = jnp.where(even, out_1[...], out_0[...])
    out_b[...] = jnp.where(even, out_0[...], out_1[...])
    out_r[...] = DT * bond_force(out_c[0:24, :], m_ref, par_ref)
    for m in range(MAXCOV):
        mom = moment(fcell[m])
        react = DT * (cs[m] * mom[3:4] - mom)
        for c in range(3):
            out_r[c * 8 + m : c * 8 + m + 1, :] += react[c : c + 1, :]


def second_kernel(
    starts, t0, t1, cst, share, r0, r1, r2, r3, m_ref, par_ref,
    out_f, out_s,
    idx, cnt, smap, cs, ps, work, hot, lcell, qcell, right, qown, fpart, fcell,
):
    j = lax.axis_index("gx")
    count = cover_slots(starts, j, idx, smap, cnt)
    ps[0:24, :] = cst[0:24, :]
    ps[24:48, :] = cst[24:48, :] + share[...]
    for m in range(MAXCOV):
        cell = idx[m]
        s = starts[cell]
        for k, (shift, ref) in enumerate(((-2, r0), (-1, r1), (1, r2), (2, r3))):
            slot = smap[k * SLABS + cell]
            there = (m < count) & (s <= j + shift) & (j + shift < s + SPAN)
            for c in range(3):
                at = 24 + c * 8 + m
                got = ref[pl.ds(c * 8 + slot, 1), :]
                ps[at : at + 1, :] += jnp.where(there, got, 0.0)
    ps[0:24, :] += DT * ps[24:48, :]
    for m in range(MAXCOV):
        cs[m] = jnp.zeros((8, NVP), F32)
        for c in range(6):
            cs[m, c : c + 1, :] = ps[c * 8 + m : c * 8 + m + 1, :]
    own = own_frame(t0, t1)
    out_f[...] = membrane(own, count, cs, work, hot, lcell, qcell, right, qown, fpart, fcell)
    bond = DT * bond_force(ps[0:24, :], m_ref, par_ref)
    out_s[...] = jnp.zeros(out_s.shape, F32)
    row = row_ids(NVP)
    shift = jnp.where(row == 1, (j * TF).astype(F32), jnp.where(row == 2, ZMID, 0.0))
    for m in range(MAXCOV):
        cell = idx[m]
        mom = moment(fcell[m])
        react = DT * (cs[m] * mom[3:4] - mom)
        push = pltpu.roll(jnp.where(row < 3, react, 0.0), 3, 0)
        whole = push + jnp.where(starts[cell] == j, cs[m] + shift, 0.0)
        for c in range(3):
            cs[m, c + 3 : c + 4, :] = bond[c * 8 + m : c * 8 + m + 1, :]
        whole = whole + jnp.where((row >= 3) & (row < 6), cs[m], 0.0)

        @pl.when(m < count)
        def _():
            for k in range(4):
                out_s[cell, k * 6 : k * 6 + 6, :] = whole[0:6, k * LANES : (k + 1) * LANES]


def late_kernel(t0, t1, in_a, in_b, gl, gh, memb, out_p, out_v, lfeat, fpart):
    own = solvent(near_frames(t0, t1, in_a, in_b, gl, gh), lfeat, fpart)
    force = memb[...] + force_of(own, fpart)
    for w, ref in enumerate((t0, t1)):
        for f in range(TF):
            t = w * TF + f
            st = moved(ref[0, f], force[:, t * LANES : (t + 1) * LANES])
            for c in range(3):
                out_p[c, w, f : f + 1, :] = st[c : c + 1]
                out_v[c, w, f : f + 1, :] = st[c + 3 : c + 4]


def vmem():
    return pl.BlockSpec(memory_space=pltpu.VMEM)


def smem():
    return pl.BlockSpec(memory_space=pltpu.SMEM)


def slot_scratch(extra):
    return (
        [pltpu.SMEM((8,), jnp.int32), pltpu.SMEM((1,), jnp.int32)]
        + extra
        + [
            pltpu.SMEM((48,), jnp.int32),
            pltpu.VMEM((2, 4 * LANES, 4 * LANES), BF16),
            pltpu.VMEM((MAXCOV, NVP, 64), BF16),
            pltpu.VMEM((MAXCOV, 32, NVP), BF16),
            pltpu.VMEM((9, 64, 2 * LANES), BF16),
            pltpu.VMEM((9, 32, 2 * LANES), BF16),
            pltpu.VMEM((9, 32, LANES), F32),
            pltpu.VMEM((8, 32, NVP), F32),
        ]
    )


def solvent_scratch():
    return [pltpu.VMEM((24 * LANES, 64), BF16), pltpu.VMEM((32, 8 * LANES), F32)]


def call(kernel, outs, scratch, args, scalars=0):
    return pl.pallas_call(
        kernel,
        out_shape=tuple(jax.ShapeDtypeStruct(s, t) for s, t in outs),
        in_specs=[smem()] * scalars + [vmem()] * (len(args) - scalars),
        out_specs=tuple(vmem() for _ in outs),
        scratch_shapes=scratch,
    )(*args)


def moves(axis, shift):
    count = lax.axis_size(axis)
    return [(k, k + shift) for k in range(count) if 0 <= k + shift < count]


def swap(out_a, out_b):
    count = lax.axis_size("wa")
    odd_pairs = [(k, k - 1 if k % 2 == 0 else k + 1) for k in range(1, count - 1)]
    in_a = lax.ppermute(out_a, "wa", [(k, k ^ 1) for k in range(count)])
    return in_a, lax.ppermute(out_b, "wa", odd_pairs)


def columns(t0, t1, in_a, in_b):
    even = lax.axis_index("wa") % 2 == 0

    def column(f):
        a, b = in_a[:, f], in_b[:, f]
        return jnp.concatenate(
            [jnp.where(even, b, a), t0[:, f], t1[:, f], jnp.where(even, a, b)], 0
        )

    gl = lax.ppermute(column(TF - 1), "gx", moves("gx", 1))
    gh = lax.ppermute(column(0), "gx", moves("gx", -1))
    return gl, gh


def body(
    part_pos, part_vel, random_kicks, vert_pos, vert_vel,
    cover_start, bond_ends, triangles, rest_len, rest_area,
):
    cell = jnp.concatenate(
        [
            jnp.pad(vert_pos[:, 0], ((0, 0), (0, NVP - NV)), constant_values=FAR),
            jnp.pad(vert_vel[:, 0], ((0, 0), (0, NVP - NV))),
        ],
        0,
    )
    cell = jnp.transpose(cell.reshape(6, 4, LANES), (1, 0, 2)).reshape(24, LANES)
    cells = lax.all_to_all(
        jnp.broadcast_to(cell[None], (SLABS, 24, LANES)), "gx", 0, 0, tiled=True
    )
    tiles = jnp.transpose(
        jnp.concatenate([part_pos, part_vel, random_kicks[0:2]], 0), (1, 2, 0, 3)
    )
    t0, t1 = tiles[:1], tiles[1:]
    even = lax.axis_index("wa") % 2 == 0
    kicks = jnp.transpose(random_kicks[2:4], (1, 2, 0, 3))
    part = ((8, TW * TF * LANES), F32)
    row = ((1, TF, 8, LANES), F32)
    wide = SPAN * NBP
    ids = jnp.concatenate(
        [
            jnp.pad(bond_ends.T, ((0, 0), (0, wide - NB)), constant_values=-1),
            jnp.pad(triangles.T, ((0, 0), (0, wide - NT)), constant_values=-1),
        ],
        0,
    )
    rests = jnp.stack(
        [
            jnp.pad(rest_len, (0, wide - NB), constant_values=1.0),
            jnp.pad(rest_area, (0, wide - NT), constant_values=1.0),
        ]
    )
    incidence, par = call(
        incidence_kernel, [((NVP, COLS), BF16), ((4, NBP), F32)], [], (ids, rests)
    )
    sides = (jnp.where(even, t1, t0), jnp.where(even, t0, t1))
    swapped = swap(*sides)
    ends = columns(t0, t1, *swapped)
    (solv,) = call(early_kernel, [part], solvent_scratch(), (t0, t1, *swapped, *ends))
    cell_scratch = pltpu.VMEM((8, 8, NVP), F32)
    n0, n1, n_a, n_b, cst, share = call(
        first_kernel,
        [row, row, row, row, ((48, NVP), F32), ((24, NVP), F32)],
        slot_scratch([cell_scratch]),
        (cover_start, t0, t1, kicks, cells, solv, incidence, par),
        1,
    )
    swapped = swap(n_a, n_b)
    got = [lax.ppermute(share, "gx", moves("gx", -s)) for s in (-2, -1, 1, 2)]
    memb, sends = call(
        second_kernel,
        [part, ((SLABS, 24, LANES), F32)],
        slot_scratch(
            [pltpu.SMEM((4 * SLABS,), jnp.int32), cell_scratch, pltpu.VMEM((48, NVP), F32)]
        ),
        (cover_start, n0, n1, cst, share, *got, incidence, par),
        1,
    )
    final = jnp.sum(lax.all_to_all(sends, "gx", 0, 0, tiled=True), 0)
    out_pos, out_vel = call(
        late_kernel,
        [((3, TW, TF, LANES), F32)] * 2,
        solvent_scratch(),
        (n0, n1, *swapped, *columns(n0, n1, *swapped), memb),
    )
    final = jnp.transpose(final.reshape(4, 6, LANES), (1, 0, 2)).reshape(6, NVP)
    new_vel = final[3:6, None, :NV]
    new_pos = final[0:3, None, :NV] + DT * new_vel
    return out_pos, out_vel, new_pos, new_vel


def solution(mesh):
    in_specs = (
        P(None, "wa", "gx", None),
        P(None, "wa", "gx", None),
        P(None, "wa", "gx", None),
        P(None, ("wa", "gx"), None),
        P(None, ("wa", "gx"), None),
        P("wa"),
        P(),
        P(),
        P(),
        P(),
    )
    out_specs = (
        P(None, "wa", "gx", None),
        P(None, "wa", "gx", None),
        P(None, ("wa", "gx"), None),
        P(None, ("wa", "gx"), None),
    )
    return jax.shard_map(body, mesh=mesh, in_specs=in_specs, out_specs=out_specs, check_vma=False)
```

```python
import jax
import jax.numpy as jnp
from jax import lax
from jax.experimental import pallas as pl
from jax.experimental.pallas import tpu as pltpu
from jax.sharding import PartitionSpec as P


SPAN = 3
MAXCOV = 5
DT = 0.04
FAR = 1000.0
ZMID = 16.0
NOISE = 15.0 * 0.7071067811865476
TW = 2
TF = 4
LANES = 128
NV = 498
NVP = 512
NB = 1488
NBP = 512
NT = 992
NTP = 384
COLS = NBP + 2 * NTP
SLABS = 32
WIDTH = 2
ROWS = 16

F32 = jnp.float32
BF16 = jnp.bfloat16


def nn(a, b):
    return lax.dot_general(a, b, (((1,), (0,)), ((), ())), preferred_element_type=F32)


def nt(a, b):
    return lax.dot_general(a, b, (((1,), (1,)), ((), ())), preferred_element_type=F32)


def split3(x):
    a = x.astype(BF16).astype(F32)
    r = x - a
    b = r.astype(BF16).astype(F32)
    return a, b, r - b


def row_ids(n):
    return lax.broadcasted_iota(jnp.int32, (8, n), 0)


def rows_of(pieces, n):
    row = row_ids(n)
    out = jnp.zeros((8, n), F32)
    for r, piece in pieces:
        out = jnp.where(row == r, piece, out)
    return out


def dots(st, n):
    row = row_ids(n)
    vel = pltpu.roll(st, 5, 0)
    sq = jnp.sum(jnp.where(row < 3, st * st, 0.0), 0, keepdims=True)
    xv = jnp.sum(jnp.where(row < 3, st * vel, 0.0), 0, keepdims=True)
    return vel, sq, xv


def left_features(st):
    n = st.shape[1]
    a, b, c = split3(st)
    _, sq, xv = dots(st, n)
    s1, s2, s3 = split3(1.0 - sq)
    v1, v2, v3 = split3(xv)
    e1 = rows_of([(0, s1), (1, s2), (2, s3), (3, v1), (4, v2), (5, v3), (6, 1.0), (7, 1.0)], n)
    e2 = rows_of([(0, 1.0)], n)
    return jnp.concatenate([a, a, a, b, b, c, e1, e2], 0)


def right_features(st):
    n = st.shape[1]
    row = row_ids(n)
    vel, sq, xv = dots(st, n)
    s1, s2, s3 = split3(-sq)
    v1, v2, v3 = split3(4.5 * xv)

    def pack(block, e1, e2):
        a, b, c = split3(block)
        return jnp.concatenate([a, b, c, a, b, a, e1, e2], 0).astype(BF16)

    zero = jnp.zeros((8, n), F32)
    near = pack(
        jnp.where(row < 3, 2.0 * st, 0.0),
        rows_of([(0, 1.0), (1, 1.0), (2, 1.0), (6, s1), (7, s2)], n),
        rows_of([(0, s3)], n),
    )
    pos = pltpu.roll(st, 3, 0)
    drag = pack(
        -4.5 * jnp.where(row < 3, vel, jnp.where(row < 6, pos, 0.0)),
        rows_of([(3, 4.5), (4, 4.5), (5, 4.5), (6, v1), (7, v2)], n),
        rows_of([(0, v3)], n),
    )
    up = pltpu.roll(st, 7, 0)
    down = pltpu.roll(st, 1, 0)
    kick = pack(
        NOISE * jnp.where(row == 6, up, jnp.where(row == 7, down, 0.0)),
        rows_of([(6, 25.0)], n),
        zero,
    )
    return near, drag, kick


def sum_features(st):
    n = st.shape[1]
    row = row_ids(n)
    q = jnp.where(row < 3, st, jnp.where(row == 3, 1.0, 0.0))
    a, b, c = split3(q)
    return jnp.concatenate([a, b, c, jnp.zeros((8, n), F32)], 0).astype(BF16)


def halves(s):
    hi = s.astype(BF16)
    return hi, (s - hi.astype(F32)).astype(BF16)


def moment(acc):
    return acc[0:8] + acc[8:16] + acc[16:24]


def cover_slots(starts, j, idx, slot_map, count_ref):
    for m in range(8):
        idx[m] = 0
    count = jnp.int32(0)
    shifts = (-2, -1, 1, 2)
    counts = [jnp.int32(0) for _ in shifts]
    for c in range(SLABS):
        s = starts[c]
        idx[jnp.minimum(count, 7)] = c
        covered = (s <= j) & (j < s + SPAN)
        count = count + covered.astype(jnp.int32)
        if slot_map is not None:
            for k, shift in enumerate(shifts):
                slot_map[k * SLABS + c] = jnp.minimum(counts[k], MAXCOV - 1)
                cov = (s <= j + shift) & (j + shift < s + SPAN)
                counts[k] = counts[k] + cov.astype(jnp.int32)
    count = jnp.minimum(count, MAXCOV)
    count_ref[0] = count
    return count


def bond_force(pos, m_ref, par):
    p3 = jnp.concatenate(split3(pos), 0).astype(BF16)

    def fold(x):
        return x[0:24] + x[24:48] + x[48:72]

    def back(g, cols):
        g3 = jnp.concatenate(split3(g), 0).astype(BF16)
        return fold(nt(g3, m_ref[:, cols]))

    one, two, three = slice(0, NBP), slice(NBP, NBP + NTP), slice(NBP + NTP, COLS)
    d = fold(nn(p3, m_ref[:, one]))
    stretch = d[0:8] * d[0:8] + d[8:16] * d[8:16] + d[16:24] * d[16:24]
    coef = (stretch - par[0:1, :]) * par[1:2, :]
    force = back(jnp.concatenate([coef * d[0:8], coef * d[8:16], coef * d[16:24]], 0), one)
    e1 = fold(nn(p3, m_ref[:, two]))
    e2 = fold(nn(p3, m_ref[:, three]))

    def cross(a, b):
        ax, ay, az = a
        bx, by, bz = b
        return ay * bz - az * by, az * bx - ax * bz, ax * by - ay * bx

    a = (e1[0:8], e1[8:16], e1[16:24])
    b = (e2[0:8], e2[8:16], e2[16:24])
    n = cross(a, b)
    area = 0.25 * (n[0] * n[0] + n[1] * n[1] + n[2] * n[2])
    coef = (area - par[2:3, :NTP]) * par[3:4, :NTP]
    g = (coef * n[0], coef * n[1], coef * n[2])
    force = force + back(jnp.concatenate(cross(b, g), 0), two)
    return force + back(jnp.concatenate(cross(g, a), 0), three)


def solvent(own, others, runs, lfeat, fpart):
    ra, rc, rb = right_features(own)
    lfeat[...] = left_features(others).T.astype(BF16)
    qnear = sum_features(others)
    for t in range(TW * TF):
        cols = slice(t * LANES, (t + 1) * LANES)
        rt = jnp.concatenate([ra[:, cols], rc[:, cols], rb[:, cols]], 1)
        spans = [(a * LANES, (a + n) * LANES) for a, n in runs[t]]
        out = nn(jnp.concatenate([lfeat[a:b, :] for a, b in spans], 0), rt)
        weight = jnp.maximum(out[:, :LANES], 0.0)
        s = weight * (out[:, 2 * LANES :] - weight * out[:, LANES : 2 * LANES])
        q = jnp.concatenate([qnear[:, a:b] for a, b in spans], 1)
        acc = nn(q, jnp.concatenate(halves(s), 1))
        fpart[:, cols] = acc[:, :LANES] + acc[:, LANES:]


def all_runs():
    return [[((w + dw) * (TF + 2) + f, 3) for dw in range(3)] for w in range(TW) for f in range(TF)]


def inner_runs():
    out = []
    for _ in range(TW):
        for f in range(TF):
            first, last = max(f - 1, 0), min(f + 1, TF - 1)
            out.append([(v * TF + first, last - first + 1) for v in range(TW)])
    return out


def outer_tiles(near):
    wide = TF + 2
    rows = near[:wide] + near[-wide:]
    return rows + [near[(w + 1) * wide] for w in range(TW)] + [near[(w + 2) * wide - 1] for w in range(TW)]


def outer_runs():
    wide = TF + 2
    out = []
    for w in range(TW):
        for f in range(TF):
            run = [(w * wide + f, 3)]
            if f == 0:
                run.append((2 * wide, TW))
            if f == TF - 1:
                run.append((2 * wide + TW, TW))
            out.append(run)
    return out


def own_of(near):
    return jnp.concatenate(
        [near[(w + 1) * (TF + 2) + f + 1] for w in range(TW) for f in range(TF)], 1
    )


def sort_half(st, hot):
    n = st.shape[1]
    z = st[2:3, :]
    column = jnp.broadcast_to(z, (8, n)).T[:, 0:1]
    ranks = []
    for k in range(n // LANES):
        cols = slice(k * LANES, (k + 1) * LANES)
        zj = z[:, cols]
        count = jnp.zeros((1, LANES), F32)
        for b in range(n // LANES):
            zi = column[b * LANES : (b + 1) * LANES]
            if b < k:
                less = zi <= zj
            elif b > k:
                less = zi < zj
            else:
                first = lax.broadcasted_iota(jnp.int32, (LANES, LANES), 0)
                second = lax.broadcasted_iota(jnp.int32, (LANES, LANES), 1)
                less = (zi < zj) | ((zi == zj) & (first < second))
            count = count + jnp.sum(jnp.where(less, 1.0, 0.0), 0, keepdims=True)
        ranks.append(count)
    rank = jnp.concatenate(ranks, 1).astype(jnp.int32)
    place = lax.broadcasted_iota(jnp.int32, (n, n), 0)
    hot[...] = jnp.where(place == rank, 1.0, 0.0).astype(BF16)
    parts = nt(jnp.concatenate(split3(st), 0).astype(BF16), hot[...])
    return parts[0:8] + parts[8:16] + parts[16:24]


def unsort_half(force, hot):
    parts = nn(jnp.concatenate(split3(force), 0).astype(BF16), hot[...])
    return parts[0:8] + parts[8:16] + parts[16:24]


def membrane(own, count, cs, work, hot, lcell, qcell, right, qown, fpart, fcell):
    order = [[w * TF + f for w in range(TW) for f in (2 * g, 2 * g + 1)] for g in range(2)]
    halves_of = [
        sort_half(jnp.concatenate([own[:, t * LANES : (t + 1) * LANES] for t in o], 1), hot.at[g])
        for g, o in enumerate(order)
    ]
    st = jnp.concatenate(halves_of, 1)
    ra, rc, _ = right_features(st)
    q = sum_features(st)
    lane = lax.broadcasted_iota(jnp.int32, (8, LANES), 1)
    low = jnp.full((8, LANES), 3.0e4, F32)
    high = -low
    for k in range(8):
        cols = slice(k * LANES, (k + 1) * LANES)
        right[k] = jnp.concatenate([ra[:, cols], rc[:, cols]], 1)
        qown[k] = jnp.concatenate([q[:, cols], q[:, cols]], 1)
        block = st[:, cols]
        low = jnp.where(lane == k, jnp.min(block, 1, keepdims=True), low)
        high = jnp.where(lane == k, jnp.max(block, 1, keepdims=True), high)
    row = row_ids(LANES)
    bits = jnp.zeros((8, LANES), F32)
    for k in range(8):
        bits = jnp.where(lane == k, float(1 << k), bits)
    real = lax.broadcasted_iota(jnp.int32, (8, NVP), 1) < NV
    right[8] = jnp.zeros((64, 2 * LANES), BF16)
    qown[8] = jnp.zeros((32, 2 * LANES), BF16)
    n = jnp.int32(0)
    for m in range(MAXCOV):
        cell = cs[m]
        cell_low = jnp.min(jnp.where(real, cell, 3.0e4), 1, keepdims=True)
        cell_high = jnp.max(jnp.where(real, cell, -3.0e4), 1, keepdims=True)
        apart = (low - 1.01 > cell_high) | (high + 1.01 < cell_low)
        apart = jnp.max(jnp.where((row < 3) & apart, 1.0, 0.0), 0, keepdims=True)
        mask = jnp.sum(jnp.where(apart > 0.5, 0.0, bits[0:1])).astype(jnp.int32)
        mask = jnp.where(m < count, mask, 0)
        for k in range(8):
            work[n] = m * 16 + k
            n = n + ((mask >> k) & 1)
    for k in range(WIDTH):
        work[n + k] = 8
    fpart[...] = jnp.zeros(fpart.shape, F32)
    fcell[...] = jnp.zeros(fcell.shape, F32)

    def one_cell(m, carry):
        lcell[m] = left_features(cs[m]).T.astype(BF16)
        qcell[m] = sum_features(cs[m])
        return carry

    lax.fori_loop(0, count, one_cell, 0)

    def some_blocks(i, carry):
        found = []
        for u in range(WIDTH):
            item = work[i * WIDTH + u]
            m, k = item >> 4, item & 15
            out = nn(lcell[m], right[k])
            weight = jnp.maximum(out[:, :LANES], 0.0)
            s = weight * (4.0 - weight * out[:, LANES:])
            both = jnp.concatenate(halves(s), 1)
            found.append((m, k, nn(qcell[m], both), nt(qown[k], both)))
        for m, k, on_parts, on_cell in found:
            fpart[k] += on_parts[:, :LANES] + on_parts[:, LANES:]
            fcell[m] += on_cell
        return carry

    lax.fori_loop(0, (n + WIDTH - 1) // WIDTH, some_blocks, 0)
    force = []
    for k in range(8):
        mom = moment(fpart[k])
        block = st[:, k * LANES : (k + 1) * LANES]
        force.append(jnp.where(row < 3, block * mom[3:4] - mom, 0.0))
    tiles = [None] * 8
    for g, o in enumerate(order):
        whole = unsort_half(jnp.concatenate(force[4 * g : 4 * g + 4], 1), hot.at[g])
        for place, t in enumerate(o):
            tiles[t] = whole[:, place * LANES : (place + 1) * LANES]
    return jnp.concatenate(tiles, 1)


def force_of(own, fpart):
    mom = moment(fpart[...])
    return jnp.where(row_ids(own.shape[1]) < 3, own * mom[3:4] - mom, 0.0)


def moved(tile, force):
    st = tile + pltpu.roll(DT * force, 3, 0)
    vel = pltpu.roll(st, 5, 0)
    return st + jnp.where(row_ids(LANES) < 3, DT * vel, 0.0)


def own_frame(t0, t1):
    row = row_ids(LANES)
    out = []
    for w, ref in enumerate((t0, t1)):
        for f in range(TF):
            shift = jnp.where(row == 0, float(w), jnp.where(row == 1, float(f), 0.0))
            out.append(ref[0, f] + jnp.where(row == 2, -ZMID, shift))
    return jnp.concatenate(out, 1)


def near_frames(t0, t1, in_a, in_b, gl, gh):
    i = lax.axis_index("wa")
    j = lax.axis_index("gx")
    row = row_ids(LANES)
    wlo = jnp.where(i == 0, FAR, 0.0)
    whi = jnp.where(i == ROWS - 1, FAR, 0.0)
    flo = jnp.where(j == 0, FAR, 0.0)
    fhi = jnp.where(j == SLABS - 1, FAR, 0.0)
    near = []
    even = i % 2 == 0
    for w, ref in enumerate((None, t0, t1, None)):
        bad_w = wlo if w == 0 else whi if w == TW + 1 else 0.0
        for f in range(TF + 2):
            if f == 0:
                tile, bad = gl[w], bad_w + flo
            elif f == TF + 1:
                tile, bad = gh[w], bad_w + fhi
            else:
                a, b = (in_b, in_a) if w == 0 else (in_a, in_b)
                tile = jnp.where(even, a[0, f - 1], b[0, f - 1]) if ref is None else ref[0, f - 1]
                bad = bad_w
            shift = jnp.where(row == 2, -ZMID, 0.0)
            shift = jnp.where(row == 0, float(w - 1) + bad, shift)
            near.append(tile + jnp.where(row == 1, float(f - 1), shift))
    return near


def incidence_kernel(ids, rests, m_ref, par_ref):
    third = lax.axis_index("gx") % SPAN
    bonds = pl.ds(pl.multiple_of(third * NBP, LANES), NBP)
    corners = pl.ds(pl.multiple_of(third * NTP, LANES), NTP)
    vid = lax.broadcasted_iota(jnp.int32, (NVP, NBP), 0)

    def column(hi, lo):
        plus = (vid[:, : hi.shape[1]] == hi).astype(F32)
        return (plus - (vid[:, : hi.shape[1]] == lo).astype(F32)).astype(BF16)

    m_ref[:, 0:NBP] = column(ids[0:1, bonds], ids[1:2, bonds])
    m_ref[:, NBP : NBP + NTP] = column(ids[3:4, corners], ids[2:3, corners])
    m_ref[:, NBP + NTP : COLS] = column(ids[4:5, corners], ids[2:3, corners])
    sq = rests[0:1, bonds] * rests[0:1, bonds]
    par_ref[0:1, :] = sq
    par_ref[1:2, :] = -2.0 / sq
    sq = rests[1:2, corners] * rests[1:2, corners]
    par_ref[2:3, 0:NTP] = sq
    par_ref[3:4, 0:NTP] = -0.125 / sq
    par_ref[2:4, NTP:NBP] = jnp.ones((2, NBP - NTP), F32)


def early_kernel(t0, t1, in_a, in_b, gl, gh, out_f, lfeat, fpart):
    near = near_frames(t0, t1, in_a, in_b, gl, gh)
    own = own_of(near)
    solvent(own, jnp.concatenate(near, 1), all_runs(), lfeat, fpart)
    out_f[...] = force_of(own, fpart)


def lay_rows(ps, m, st):
    for c in range(6):
        ps[c * 8 + m : c * 8 + m + 1, :] = st[c : c + 1, :]


def first_kernel(
    starts, t0, t1, kicks, cells, solv, m_ref, par_ref,
    out_0, out_1, out_a, out_b, out_c, out_r,
    idx, cnt, cs, work, hot, lcell, qcell, right, qown, fpart, fcell,
):
    j = lax.axis_index("gx")
    count = cover_slots(starts, j, idx, None, cnt)
    out_c[...] = jnp.zeros((48, NVP), F32)
    row = row_ids(NVP)
    shift = jnp.where(row == 1, -(j * TF).astype(F32), jnp.where(row == 2, -ZMID, 0.0))
    away = jnp.where(row < 3, FAR, 0.0)
    for m in range(MAXCOV):
        cs[m] = jnp.zeros((8, NVP), F32)
        for k in range(4):
            cs[m, 0:6, k * LANES : (k + 1) * LANES] = cells[idx[m], k * 6 : k * 6 + 6, :]
        st = jnp.where(m < count, cs[m] + shift, away)
        cs[m] = st
        lay_rows(out_c, m, st)
    own = own_frame(t0, t1)
    force = solv[...] + membrane(own, count, cs, work, hot, lcell, qcell, right, qown, fpart, fcell)
    for w, (ref, out) in enumerate(((t0, out_0), (t1, out_1))):
        for f in range(TF):
            t = w * TF + f
            st = moved(ref[0, f], force[:, t * LANES : (t + 1) * LANES])
            out[0, f, 0:6, :] = st[0:6]
            out[0, f, 6:8, :] = kicks[w, f]
    even = lax.axis_index("wa") % 2 == 0
    out_a[...] = jnp.where(even, out_1[...], out_0[...])
    out_b[...] = jnp.where(even, out_0[...], out_1[...])
    bond = DT * bond_force(out_c[0:24, :], m_ref, par_ref)
    out_r[15:16, :] = jnp.zeros((1, NVP), F32)
    for m in range(MAXCOV):
        mom = moment(fcell[m])
        react = DT * (cs[m] * mom[3:4] - mom)
        for c in range(3):
            at = c * MAXCOV + m
            out_r[at : at + 1, :] = bond[c * 8 + m : c * 8 + m + 1, :] + react[c : c + 1, :]


def second_kernel(
    starts, t0, t1, cst, share, r0, r1, r2, r3, m_ref, par_ref,
    out_f, out_s,
    idx, cnt, smap, cs, ps, work, hot, lcell, qcell, right, qown, fpart, fcell,
):
    j = lax.axis_index("gx")
    count = cover_slots(starts, j, idx, smap, cnt)
    ps[0:24, :] = cst[0:24, :]
    ps[24:48, :] = cst[24:48, :]
    for m in range(MAXCOV):
        cell = idx[m]
        s = starts[cell]
        for c in range(3):
            at = c * MAXCOV + m
            ps[24 + c * 8 + m : 25 + c * 8 + m, :] += share[at : at + 1, :]
        for k, (shift, ref) in enumerate(((-2, r0), (-1, r1), (1, r2), (2, r3))):
            slot = smap[k * SLABS + cell]
            there = (m < count) & (s <= j + shift) & (j + shift < s + SPAN)
            for c in range(3):
                at = 24 + c * 8 + m
                got = ref[pl.ds(c * MAXCOV + slot, 1), :]
                ps[at : at + 1, :] += jnp.where(there, got, 0.0)
    ps[0:24, :] += DT * ps[24:48, :]
    for m in range(MAXCOV):
        cs[m] = jnp.zeros((8, NVP), F32)
        for c in range(6):
            cs[m, c : c + 1, :] = ps[c * 8 + m : c * 8 + m + 1, :]
    own = own_frame(t0, t1)
    out_f[...] = membrane(own, count, cs, work, hot, lcell, qcell, right, qown, fpart, fcell)
    bond = DT * bond_force(ps[0:24, :], m_ref, par_ref)
    out_s[...] = jnp.zeros(out_s.shape, F32)
    row = row_ids(NVP)
    shift = jnp.where(row == 1, (j * TF).astype(F32), jnp.where(row == 2, ZMID, 0.0))
    for m in range(MAXCOV):
        cell = idx[m]
        mom = moment(fcell[m])
        react = DT * (cs[m] * mom[3:4] - mom)
        push = pltpu.roll(jnp.where(row < 3, react, 0.0), 3, 0)
        whole = push + jnp.where(starts[cell] == j, cs[m] + shift, 0.0)
        for c in range(3):
            cs[m, c + 3 : c + 4, :] = bond[c * 8 + m : c * 8 + m + 1, :]
        whole = whole + jnp.where((row >= 3) & (row < 6), cs[m], 0.0)

        @pl.when(m < count)
        def _():
            for k in range(4):
                out_s[cell, k * 6 : k * 6 + 6, :] = whole[0:6, k * LANES : (k + 1) * LANES]


def inner_kernel(t0, t1, memb, out_f, lfeat, fpart):
    own = own_frame(t0, t1)
    solvent(own, own, inner_runs(), lfeat, fpart)
    out_f[...] = memb[...] + force_of(own, fpart)


def late_kernel(t0, t1, in_a, in_b, gl, gh, memb, out_p, out_v, lfeat, fpart):
    near = near_frames(t0, t1, in_a, in_b, gl, gh)
    own = own_of(near)
    solvent(own, jnp.concatenate(outer_tiles(near), 1), outer_runs(), lfeat, fpart)
    force = memb[...] + force_of(own, fpart)
    for w, ref in enumerate((t0, t1)):
        for f in range(TF):
            t = w * TF + f
            st = moved(ref[0, f], force[:, t * LANES : (t + 1) * LANES])
            for c in range(3):
                out_p[c, w, f : f + 1, :] = st[c : c + 1]
                out_v[c, w, f : f + 1, :] = st[c + 3 : c + 4]


def vmem():
    return pl.BlockSpec(memory_space=pltpu.VMEM)


def smem():
    return pl.BlockSpec(memory_space=pltpu.SMEM)


def slot_scratch(extra):
    return (
        [pltpu.SMEM((8,), jnp.int32), pltpu.SMEM((1,), jnp.int32)]
        + extra
        + [
            pltpu.SMEM((48,), jnp.int32),
            pltpu.VMEM((2, 4 * LANES, 4 * LANES), BF16),
            pltpu.VMEM((MAXCOV, NVP, 64), BF16),
            pltpu.VMEM((MAXCOV, 32, NVP), BF16),
            pltpu.VMEM((9, 64, 2 * LANES), BF16),
            pltpu.VMEM((9, 32, 2 * LANES), BF16),
            pltpu.VMEM((9, 32, LANES), F32),
            pltpu.VMEM((8, 32, NVP), F32),
        ]
    )


def solvent_scratch(tiles):
    return [pltpu.VMEM((tiles * LANES, 64), BF16), pltpu.VMEM((32, 8 * LANES), F32)]


def call(kernel, outs, scratch, args, scalars=0):
    return pl.pallas_call(
        kernel,
        out_shape=tuple(jax.ShapeDtypeStruct(s, t) for s, t in outs),
        in_specs=[smem()] * scalars + [vmem()] * (len(args) - scalars),
        out_specs=tuple(vmem() for _ in outs),
        scratch_shapes=scratch,
    )(*args)


def moves(axis, shift):
    count = lax.axis_size(axis)
    return [(k, k + shift) for k in range(count) if 0 <= k + shift < count]


def swap(out_a, out_b):
    count = lax.axis_size("wa")
    odd_pairs = [(k, k - 1 if k % 2 == 0 else k + 1) for k in range(1, count - 1)]
    in_a = lax.ppermute(out_a, "wa", [(k, k ^ 1) for k in range(count)])
    return in_a, lax.ppermute(out_b, "wa", odd_pairs)


def columns(t0, t1, in_a, in_b):
    even = lax.axis_index("wa") % 2 == 0

    def column(f):
        a, b = in_a[:, f], in_b[:, f]
        return jnp.concatenate(
            [jnp.where(even, b, a), t0[:, f], t1[:, f], jnp.where(even, a, b)], 0
        )

    gl = lax.ppermute(column(TF - 1), "gx", moves("gx", 1))
    gh = lax.ppermute(column(0), "gx", moves("gx", -1))
    return gl, gh


def body(
    part_pos, part_vel, random_kicks, vert_pos, vert_vel,
    cover_start, bond_ends, triangles, rest_len, rest_area,
):
    cell = jnp.concatenate(
        [
            jnp.pad(vert_pos[:, 0], ((0, 0), (0, NVP - NV)), constant_values=FAR),
            jnp.pad(vert_vel[:, 0], ((0, 0), (0, NVP - NV))),
        ],
        0,
    )
    cell = jnp.transpose(cell.reshape(6, 4, LANES), (1, 0, 2)).reshape(24, LANES)
    cells = lax.all_to_all(
        jnp.broadcast_to(cell[None], (SLABS, 24, LANES)), "gx", 0, 0, tiled=True
    )
    tiles = jnp.transpose(
        jnp.concatenate([part_pos, part_vel, random_kicks[0:2]], 0), (1, 2, 0, 3)
    )
    t0, t1 = tiles[:1], tiles[1:]
    even = lax.axis_index("wa") % 2 == 0
    kicks = jnp.transpose(random_kicks[2:4], (1, 2, 0, 3))
    part = ((8, TW * TF * LANES), F32)
    row = ((1, TF, 8, LANES), F32)
    wide = SPAN * NBP
    ids = jnp.concatenate(
        [
            jnp.pad(bond_ends.T, ((0, 0), (0, wide - NB)), constant_values=-1),
            jnp.pad(triangles.T, ((0, 0), (0, wide - NT)), constant_values=-1),
        ],
        0,
    )
    rests = jnp.stack(
        [
            jnp.pad(rest_len, (0, wide - NB), constant_values=1.0),
            jnp.pad(rest_area, (0, wide - NT), constant_values=1.0),
        ]
    )
    incidence, par = call(
        incidence_kernel, [((NVP, COLS), BF16), ((4, NBP), F32)], [], (ids, rests)
    )
    sides = (jnp.where(even, t1, t0), jnp.where(even, t0, t1))
    swapped = swap(*sides)
    ends = columns(t0, t1, *swapped)
    (solv,) = call(early_kernel, [part], solvent_scratch(24), (t0, t1, *swapped, *ends))
    cell_scratch = pltpu.VMEM((8, 8, NVP), F32)
    n0, n1, n_a, n_b, cst, share = call(
        first_kernel,
        [row, row, row, row, ((48, NVP), F32), ((16, NVP), F32)],
        slot_scratch([cell_scratch]),
        (cover_start, t0, t1, kicks, cells, solv, incidence, par),
        1,
    )
    swapped = swap(n_a, n_b)
    got = [lax.ppermute(share, "gx", moves("gx", -s)) for s in (-2, -1, 1, 2)]
    memb, sends = call(
        second_kernel,
        [part, ((SLABS, 24, LANES), F32)],
        slot_scratch(
            [pltpu.SMEM((4 * SLABS,), jnp.int32), cell_scratch, pltpu.VMEM((48, NVP), F32)]
        ),
        (cover_start, n0, n1, cst, share, *got, incidence, par),
        1,
    )
    final = jnp.sum(lax.all_to_all(sends, "gx", 0, 0, tiled=True), 0)
    ends = columns(n0, n1, *swapped)
    (inner,) = call(inner_kernel, [part], solvent_scratch(8), (n0, n1, memb))
    out_pos, out_vel = call(
        late_kernel,
        [((3, TW, TF, LANES), F32)] * 2,
        solvent_scratch(16),
        (n0, n1, *swapped, *ends, inner),
    )
    final = jnp.transpose(final.reshape(4, 6, LANES), (1, 0, 2)).reshape(6, NVP)
    new_vel = final[3:6, None, :NV]
    new_pos = final[0:3, None, :NV] + DT * new_vel
    return out_pos, out_vel, new_pos, new_vel


def solution(mesh):
    in_specs = (
        P(None, "wa", "gx", None),
        P(None, "wa", "gx", None),
        P(None, "wa", "gx", None),
        P(None, ("wa", "gx"), None),
        P(None, ("wa", "gx"), None),
        P("wa"),
        P(),
        P(),
        P(),
        P(),
    )
    out_specs = (
        P(None, "wa", "gx", None),
        P(None, "wa", "gx", None),
        P(None, ("wa", "gx"), None),
        P(None, ("wa", "gx"), None),
    )
    return jax.shard_map(body, mesh=mesh, in_specs=in_specs, out_specs=out_specs, check_vma=False)
```

```python
import jax
import jax.numpy as jnp
from jax import lax
from jax.experimental import pallas as pl
from jax.experimental.pallas import tpu as pltpu
from jax.sharding import PartitionSpec as P


SPAN = 3
MAXCOV = 5
DT = 0.04
FAR = 1000.0
ZMID = 16.0
NOISE = 15.0 * 0.7071067811865476
TW = 2
TF = 4
LANES = 128
NV = 498
NVP = 512
NB = 1488
NBP = 512
NT = 992
NTP = 384
COLS = NBP + 2 * NTP
SLABS = 32
WIDTH = 2
ROWS = 16

F32 = jnp.float32
BF16 = jnp.bfloat16


def nn(a, b):
    return lax.dot_general(a, b, (((1,), (0,)), ((), ())), preferred_element_type=F32)


def nt(a, b):
    return lax.dot_general(a, b, (((1,), (1,)), ((), ())), preferred_element_type=F32)


def split3(x):
    a = x.astype(BF16).astype(F32)
    r = x - a
    b = r.astype(BF16).astype(F32)
    return a, b, r - b


def row_ids(n):
    return lax.broadcasted_iota(jnp.int32, (8, n), 0)


def rows_of(pieces, n):
    row = row_ids(n)
    out = jnp.zeros((8, n), F32)
    for r, piece in pieces:
        out = jnp.where(row == r, piece, out)
    return out


def dots(st, n):
    row = row_ids(n)
    vel = pltpu.roll(st, 5, 0)
    sq = jnp.sum(jnp.where(row < 3, st * st, 0.0), 0, keepdims=True)
    xv = jnp.sum(jnp.where(row < 3, st * vel, 0.0), 0, keepdims=True)
    return vel, sq, xv


def left_features(st):
    n = st.shape[1]
    a, b, c = split3(st)
    _, sq, xv = dots(st, n)
    s1, s2, s3 = split3(1.0 - sq)
    v1, v2, v3 = split3(xv)
    e1 = rows_of([(0, s1), (1, s2), (2, s3), (3, v1), (4, v2), (5, v3), (6, 1.0), (7, 1.0)], n)
    e2 = rows_of([(0, 1.0)], n)
    return jnp.concatenate([a, a, a, b, b, c, e1, e2], 0)


def right_features(st):
    n = st.shape[1]
    row = row_ids(n)
    vel, sq, xv = dots(st, n)
    s1, s2, s3 = split3(-sq)
    v1, v2, v3 = split3(4.5 * xv)

    def pack(block, e1, e2):
        a, b, c = split3(block)
        return jnp.concatenate([a, b, c, a, b, a, e1, e2], 0).astype(BF16)

    zero = jnp.zeros((8, n), F32)
    near = pack(
        jnp.where(row < 3, 2.0 * st, 0.0),
        rows_of([(0, 1.0), (1, 1.0), (2, 1.0), (6, s1), (7, s2)], n),
        rows_of([(0, s3)], n),
    )
    pos = pltpu.roll(st, 3, 0)
    drag = pack(
        -4.5 * jnp.where(row < 3, vel, jnp.where(row < 6, pos, 0.0)),
        rows_of([(3, 4.5), (4, 4.5), (5, 4.5), (6, v1), (7, v2)], n),
        rows_of([(0, v3)], n),
    )
    up = pltpu.roll(st, 7, 0)
    down = pltpu.roll(st, 1, 0)
    kick = pack(
        NOISE * jnp.where(row == 6, up, jnp.where(row == 7, down, 0.0)),
        rows_of([(6, 25.0)], n),
        zero,
    )
    return near, drag, kick


def sum_features(st):
    n = st.shape[1]
    row = row_ids(n)
    q = jnp.where(row < 3, st, jnp.where(row == 3, 1.0, 0.0))
    a, b, c = split3(q)
    return jnp.concatenate([a, b, c, jnp.zeros((8, n), F32)], 0).astype(BF16)


def halves(s):
    hi = s.astype(BF16)
    return hi, (s - hi.astype(F32)).astype(BF16)


def moment(acc):
    return acc[0:8] + acc[8:16] + acc[16:24]


def cover_slots(starts, j, idx, slot_map, count_ref):
    for m in range(8):
        idx[m] = 0
    count = jnp.int32(0)
    shifts = (-2, -1, 1, 2)
    counts = [jnp.int32(0) for _ in shifts]
    for c in range(SLABS):
        s = starts[c]
        idx[jnp.minimum(count, 7)] = c
        covered = (s <= j) & (j < s + SPAN)
        count = count + covered.astype(jnp.int32)
        if slot_map is not None:
            for k, shift in enumerate(shifts):
                slot_map[k * SLABS + c] = jnp.minimum(counts[k], MAXCOV - 1)
                cov = (s <= j + shift) & (j + shift < s + SPAN)
                counts[k] = counts[k] + cov.astype(jnp.int32)
    count = jnp.minimum(count, MAXCOV)
    count_ref[0] = count
    return count


def bond_force(pos, m_ref, par):
    p3 = jnp.concatenate(split3(pos), 0).astype(BF16)

    def fold(x):
        return x[0:24] + x[24:48] + x[48:72]

    def back(g, cols):
        g3 = jnp.concatenate(split3(g), 0).astype(BF16)
        return fold(nt(g3, m_ref[:, cols]))

    one, two, three = slice(0, NBP), slice(NBP, NBP + NTP), slice(NBP + NTP, COLS)
    d = fold(nn(p3, m_ref[:, one]))
    stretch = d[0:8] * d[0:8] + d[8:16] * d[8:16] + d[16:24] * d[16:24]
    coef = (stretch - par[0:1, :]) * par[1:2, :]
    force = back(jnp.concatenate([coef * d[0:8], coef * d[8:16], coef * d[16:24]], 0), one)
    e1 = fold(nn(p3, m_ref[:, two]))
    e2 = fold(nn(p3, m_ref[:, three]))

    def cross(a, b):
        ax, ay, az = a
        bx, by, bz = b
        return ay * bz - az * by, az * bx - ax * bz, ax * by - ay * bx

    a = (e1[0:8], e1[8:16], e1[16:24])
    b = (e2[0:8], e2[8:16], e2[16:24])
    n = cross(a, b)
    area = 0.25 * (n[0] * n[0] + n[1] * n[1] + n[2] * n[2])
    coef = (area - par[2:3, :NTP]) * par[3:4, :NTP]
    g = (coef * n[0], coef * n[1], coef * n[2])
    force = force + back(jnp.concatenate(cross(b, g), 0), two)
    return force + back(jnp.concatenate(cross(g, a), 0), three)


def solvent(own, others, runs, lfeat, fpart):
    ra, rc, rb = right_features(own)
    lfeat[...] = left_features(others).T.astype(BF16)
    qnear = sum_features(others)
    for t in range(TW * TF):
        cols = slice(t * LANES, (t + 1) * LANES)
        rt = jnp.concatenate([ra[:, cols], rc[:, cols], rb[:, cols]], 1)
        spans = [(a * LANES, (a + n) * LANES) for a, n in runs[t]]
        out = nn(jnp.concatenate([lfeat[a:b, :] for a, b in spans], 0), rt)
        weight = jnp.maximum(out[:, :LANES], 0.0)
        s = weight * (out[:, 2 * LANES :] - weight * out[:, LANES : 2 * LANES])
        q = jnp.concatenate([qnear[:, a:b] for a, b in spans], 1)
        acc = nn(q, jnp.concatenate(halves(s), 1))
        fpart[:, cols] = acc[:, :LANES] + acc[:, LANES:]


def all_runs():
    return [[((w + dw) * (TF + 2) + f, 3) for dw in range(3)] for w in range(TW) for f in range(TF)]


def inner_runs():
    out = []
    for _ in range(TW):
        for f in range(TF):
            first, last = max(f - 1, 0), min(f + 1, TF - 1)
            out.append([(v * TF + first, last - first + 1) for v in range(TW)])
    return out


def outer_tiles(near):
    wide = TF + 2
    rows = near[:wide] + near[-wide:]
    return rows + [near[(w + 1) * wide] for w in range(TW)] + [near[(w + 2) * wide - 1] for w in range(TW)]


def outer_runs():
    wide = TF + 2
    out = []
    for w in range(TW):
        for f in range(TF):
            run = [(w * wide + f, 3)]
            if f == 0:
                run.append((2 * wide, TW))
            if f == TF - 1:
                run.append((2 * wide + TW, TW))
            out.append(run)
    return out


def own_of(near):
    return jnp.concatenate(
        [near[(w + 1) * (TF + 2) + f + 1] for w in range(TW) for f in range(TF)], 1
    )


def sort_half(st, hot):
    n = st.shape[1]
    z = st[2:3, :]
    column = jnp.broadcast_to(z, (8, n)).T[:, 0:1]
    ranks = []
    for k in range(n // LANES):
        cols = slice(k * LANES, (k + 1) * LANES)
        zj = z[:, cols]
        count = jnp.zeros((1, LANES), F32)
        for b in range(n // LANES):
            zi = column[b * LANES : (b + 1) * LANES]
            if b < k:
                less = zi <= zj
            elif b > k:
                less = zi < zj
            else:
                first = lax.broadcasted_iota(jnp.int32, (LANES, LANES), 0)
                second = lax.broadcasted_iota(jnp.int32, (LANES, LANES), 1)
                less = (zi < zj) | ((zi == zj) & (first < second))
            count = count + jnp.sum(jnp.where(less, 1.0, 0.0), 0, keepdims=True)
        ranks.append(count)
    rank = jnp.concatenate(ranks, 1).astype(jnp.int32)
    place = lax.broadcasted_iota(jnp.int32, (n, n), 0)
    hot[...] = jnp.where(place == rank, 1.0, 0.0).astype(BF16)
    parts = nt(jnp.concatenate(split3(st), 0).astype(BF16), hot[...])
    return parts[0:8] + parts[8:16] + parts[16:24]


def unsort_half(force, hot):
    parts = nn(jnp.concatenate(split3(force), 0).astype(BF16), hot[...])
    return parts[0:8] + parts[8:16] + parts[16:24]


def membrane(own, count, cs, work, hot, lcell, qcell, right, qown, fpart, fcell):
    order = [[w * TF + f for w in range(TW) for f in (2 * g, 2 * g + 1)] for g in range(2)]
    halves_of = [
        sort_half(jnp.concatenate([own[:, t * LANES : (t + 1) * LANES] for t in o], 1), hot.at[g])
        for g, o in enumerate(order)
    ]
    st = jnp.concatenate(halves_of, 1)
    ra, rc, _ = right_features(st)
    q = sum_features(st)
    lane = lax.broadcasted_iota(jnp.int32, (8, LANES), 1)
    low = jnp.full((8, LANES), 3.0e4, F32)
    high = -low
    for k in range(8):
        cols = slice(k * LANES, (k + 1) * LANES)
        right[k] = jnp.concatenate([ra[:, cols], rc[:, cols]], 1)
        qown[k] = jnp.concatenate([q[:, cols], q[:, cols]], 1)
        block = st[:, cols]
        low = jnp.where(lane == k, jnp.min(block, 1, keepdims=True), low)
        high = jnp.where(lane == k, jnp.max(block, 1, keepdims=True), high)
    row = row_ids(LANES)
    bits = jnp.zeros((8, LANES), F32)
    for k in range(8):
        bits = jnp.where(lane == k, float(1 << k), bits)
    real = lax.broadcasted_iota(jnp.int32, (8, NVP), 1) < NV
    right[8] = jnp.zeros((64, 2 * LANES), BF16)
    qown[8] = jnp.zeros((32, 2 * LANES), BF16)
    n = jnp.int32(0)
    for m in range(MAXCOV):
        cell = cs[m]
        cell_low = jnp.min(jnp.where(real, cell, 3.0e4), 1, keepdims=True)
        cell_high = jnp.max(jnp.where(real, cell, -3.0e4), 1, keepdims=True)
        apart = (low - 1.01 > cell_high) | (high + 1.01 < cell_low)
        apart = jnp.max(jnp.where((row < 3) & apart, 1.0, 0.0), 0, keepdims=True)
        mask = jnp.sum(jnp.where(apart > 0.5, 0.0, bits[0:1])).astype(jnp.int32)
        mask = jnp.where(m < count, mask, 0)
        for k in range(8):
            work[n] = m * 16 + k
            n = n + ((mask >> k) & 1)
    for k in range(WIDTH):
        work[n + k] = 8
    fpart[...] = jnp.zeros(fpart.shape, F32)
    fcell[...] = jnp.zeros(fcell.shape, F32)

    def one_cell(m, carry):
        lcell[m] = left_features(cs[m]).T.astype(BF16)
        qcell[m] = sum_features(cs[m])
        return carry

    lax.fori_loop(0, count, one_cell, 0)

    def some_blocks(i, carry):
        found = []
        for u in range(WIDTH):
            item = work[i * WIDTH + u]
            m, k = item >> 4, item & 15
            out = nn(lcell[m], right[k])
            weight = jnp.maximum(out[:, :LANES], 0.0)
            s = weight * (4.0 - weight * out[:, LANES:])
            both = jnp.concatenate(halves(s), 1)
            found.append((m, k, nn(qcell[m], both), nt(qown[k], both)))
        for m, k, on_parts, on_cell in found:
            fpart[k] += on_parts[:, :LANES] + on_parts[:, LANES:]
            fcell[m] += on_cell
        return carry

    lax.fori_loop(0, (n + WIDTH - 1) // WIDTH, some_blocks, 0)
    force = []
    for k in range(8):
        mom = moment(fpart[k])
        block = st[:, k * LANES : (k + 1) * LANES]
        force.append(jnp.where(row < 3, block * mom[3:4] - mom, 0.0))
    tiles = [None] * 8
    for g, o in enumerate(order):
        whole = unsort_half(jnp.concatenate(force[4 * g : 4 * g + 4], 1), hot.at[g])
        for place, t in enumerate(o):
            tiles[t] = whole[:, place * LANES : (place + 1) * LANES]
    return jnp.concatenate(tiles, 1)


def force_of(own, fpart):
    mom = moment(fpart[...])
    return jnp.where(row_ids(own.shape[1]) < 3, own * mom[3:4] - mom, 0.0)


def moved(tile, force):
    st = tile + pltpu.roll(DT * force, 3, 0)
    vel = pltpu.roll(st, 5, 0)
    return st + jnp.where(row_ids(LANES) < 3, DT * vel, 0.0)


def own_frame(t0, t1):
    row = row_ids(LANES)
    out = []
    for w, ref in enumerate((t0, t1)):
        for f in range(TF):
            shift = jnp.where(row == 0, float(w), jnp.where(row == 1, float(f), 0.0))
            out.append(ref[0, f] + jnp.where(row == 2, -ZMID, shift))
    return jnp.concatenate(out, 1)


def near_frames(t0, t1, in_a, in_b, gl, gh):
    i = lax.axis_index("wa")
    j = lax.axis_index("gx")
    row = row_ids(LANES)
    wlo = jnp.where(i == 0, FAR, 0.0)
    whi = jnp.where(i == ROWS - 1, FAR, 0.0)
    flo = jnp.where(j == 0, FAR, 0.0)
    fhi = jnp.where(j == SLABS - 1, FAR, 0.0)
    near = []
    even = i % 2 == 0
    for w, ref in enumerate((None, t0, t1, None)):
        bad_w = wlo if w == 0 else whi if w == TW + 1 else 0.0
        for f in range(TF + 2):
            if f == 0:
                tile, bad = gl[w], bad_w + flo
            elif f == TF + 1:
                tile, bad = gh[w], bad_w + fhi
            else:
                a, b = (in_b, in_a) if w == 0 else (in_a, in_b)
                tile = jnp.where(even, a[0, f - 1], b[0, f - 1]) if ref is None else ref[0, f - 1]
                bad = bad_w
            shift = jnp.where(row == 2, -ZMID, 0.0)
            shift = jnp.where(row == 0, float(w - 1) + bad, shift)
            near.append(tile + jnp.where(row == 1, float(f - 1), shift))
    return near


def incidence_kernel(bond_ids, corner_ids, rest_len, rest_area, m_ref, par_ref, ids, rests):
    ids[...] = jnp.full(ids.shape, -1, jnp.int32)
    rests[...] = jnp.ones(rests.shape, F32)
    ids[0:2, 0:NB] = bond_ids[...]
    ids[2:5, 0:NT] = corner_ids[...]
    rests[0:1, 0:NB] = rest_len[...]
    rests[1:2, 0:NT] = rest_area[...]
    third = lax.axis_index("gx") % SPAN
    bonds = pl.ds(pl.multiple_of(third * NBP, LANES), NBP)
    corners = pl.ds(pl.multiple_of(third * NTP, LANES), NTP)
    vid = lax.broadcasted_iota(jnp.int32, (NVP, NBP), 0)

    def column(hi, lo):
        plus = (vid[:, : hi.shape[1]] == hi).astype(F32)
        return (plus - (vid[:, : hi.shape[1]] == lo).astype(F32)).astype(BF16)

    m_ref[:, 0:NBP] = column(ids[0:1, bonds], ids[1:2, bonds])
    m_ref[:, NBP : NBP + NTP] = column(ids[3:4, corners], ids[2:3, corners])
    m_ref[:, NBP + NTP : COLS] = column(ids[4:5, corners], ids[2:3, corners])
    sq = rests[0:1, bonds] * rests[0:1, bonds]
    par_ref[0:1, :] = sq
    par_ref[1:2, :] = -2.0 / sq
    sq = rests[1:2, corners] * rests[1:2, corners]
    par_ref[2:3, 0:NTP] = sq
    par_ref[3:4, 0:NTP] = -0.125 / sq
    par_ref[2:4, NTP:NBP] = jnp.ones((2, NBP - NTP), F32)


def early_kernel(t0, t1, in_a, in_b, gl, gh, out_f, lfeat, fpart):
    near = near_frames(t0, t1, in_a, in_b, gl, gh)
    own = own_of(near)
    solvent(own, jnp.concatenate(near, 1), all_runs(), lfeat, fpart)
    out_f[...] = force_of(own, fpart)


def lay_rows(ps, m, st):
    for c in range(6):
        ps[c * 8 + m : c * 8 + m + 1, :] = st[c : c + 1, :]


def first_kernel(
    starts, t0, t1, kicks, cells, solv, m_ref, par_ref,
    out_0, out_1, out_a, out_b, out_c, out_r,
    idx, cnt, cs, work, hot, lcell, qcell, right, qown, fpart, fcell,
):
    j = lax.axis_index("gx")
    count = cover_slots(starts, j, idx, None, cnt)
    out_c[...] = jnp.zeros((48, NVP), F32)
    row = row_ids(NVP)
    shift = jnp.where(row == 1, -(j * TF).astype(F32), jnp.where(row == 2, -ZMID, 0.0))
    away = jnp.where(row < 3, FAR, 0.0)
    for m in range(MAXCOV):
        cs[m] = jnp.zeros((8, NVP), F32)
        for k in range(4):
            cs[m, 0:6, k * LANES : (k + 1) * LANES] = cells[idx[m], k * 6 : k * 6 + 6, :]
        st = jnp.where(m < count, cs[m] + shift, away)
        cs[m] = st
        lay_rows(out_c, m, st)
    own = own_frame(t0, t1)
    force = solv[...] + membrane(own, count, cs, work, hot, lcell, qcell, right, qown, fpart, fcell)
    for w, (ref, out) in enumerate(((t0, out_0), (t1, out_1))):
        for f in range(TF):
            t = w * TF + f
            st = moved(ref[0, f], force[:, t * LANES : (t + 1) * LANES])
            out[0, f, 0:6, :] = st[0:6]
            out[0, f, 6:8, :] = kicks[w, f]
    even = lax.axis_index("wa") % 2 == 0
    out_a[...] = jnp.where(even, out_1[...], out_0[...])
    out_b[...] = jnp.where(even, out_0[...], out_1[...])
    bond = DT * bond_force(out_c[0:24, :], m_ref, par_ref)
    out_r[15:16, :] = jnp.zeros((1, NVP), F32)
    for m in range(MAXCOV):
        mom = moment(fcell[m])
        react = DT * (cs[m] * mom[3:4] - mom)
        for c in range(3):
            at = c * MAXCOV + m
            out_r[at : at + 1, :] = bond[c * 8 + m : c * 8 + m + 1, :] + react[c : c + 1, :]


def second_kernel(
    starts, t0, t1, cst, share, r0, r1, r2, r3, m_ref, par_ref,
    out_f, out_s,
    idx, cnt, smap, cs, ps, work, hot, lcell, qcell, right, qown, fpart, fcell,
):
    j = lax.axis_index("gx")
    count = cover_slots(starts, j, idx, smap, cnt)
    ps[0:24, :] = cst[0:24, :]
    ps[24:48, :] = cst[24:48, :]
    for m in range(MAXCOV):
        cell = idx[m]
        s = starts[cell]
        for c in range(3):
            at = c * MAXCOV + m
            ps[24 + c * 8 + m : 25 + c * 8 + m, :] += share[at : at + 1, :]
        for k, (shift, ref) in enumerate(((-2, r0), (-1, r1), (1, r2), (2, r3))):
            slot = smap[k * SLABS + cell]
            there = (m < count) & (s <= j + shift) & (j + shift < s + SPAN)
            for c in range(3):
                at = 24 + c * 8 + m
                got = ref[pl.ds(c * MAXCOV + slot, 1), :]
                ps[at : at + 1, :] += jnp.where(there, got, 0.0)
    ps[0:24, :] += DT * ps[24:48, :]
    for m in range(MAXCOV):
        cs[m] = jnp.zeros((8, NVP), F32)
        for c in range(6):
            cs[m, c : c + 1, :] = ps[c * 8 + m : c * 8 + m + 1, :]
    own = own_frame(t0, t1)
    out_f[...] = membrane(own, count, cs, work, hot, lcell, qcell, right, qown, fpart, fcell)
    bond = DT * bond_force(ps[0:24, :], m_ref, par_ref)
    out_s[...] = jnp.zeros(out_s.shape, F32)
    row = row_ids(NVP)
    shift = jnp.where(row == 1, (j * TF).astype(F32), jnp.where(row == 2, ZMID, 0.0))
    for m in range(MAXCOV):
        cell = idx[m]
        mom = moment(fcell[m])
        react = DT * (cs[m] * mom[3:4] - mom)
        push = pltpu.roll(jnp.where(row < 3, react, 0.0), 3, 0)
        whole = push + jnp.where(starts[cell] == j, cs[m] + shift, 0.0)
        for c in range(3):
            cs[m, c + 3 : c + 4, :] = bond[c * 8 + m : c * 8 + m + 1, :]
        whole = whole + jnp.where((row >= 3) & (row < 6), cs[m], 0.0)

        @pl.when(m < count)
        def _():
            for k in range(4):
                out_s[cell, k * 6 : k * 6 + 6, :] = whole[0:6, k * LANES : (k + 1) * LANES]


def inner_kernel(t0, t1, memb, out_f, lfeat, fpart):
    own = own_frame(t0, t1)
    solvent(own, own, inner_runs(), lfeat, fpart)
    out_f[...] = memb[...] + force_of(own, fpart)


def late_kernel(t0, t1, in_a, in_b, gl, gh, memb, out_p, out_v, lfeat, fpart):
    near = near_frames(t0, t1, in_a, in_b, gl, gh)
    own = own_of(near)
    solvent(own, jnp.concatenate(outer_tiles(near), 1), outer_runs(), lfeat, fpart)
    force = memb[...] + force_of(own, fpart)
    for w, ref in enumerate((t0, t1)):
        for f in range(TF):
            t = w * TF + f
            st = moved(ref[0, f], force[:, t * LANES : (t + 1) * LANES])
            for c in range(3):
                out_p[c, w, f : f + 1, :] = st[c : c + 1]
                out_v[c, w, f : f + 1, :] = st[c + 3 : c + 4]


def vmem():
    return pl.BlockSpec(memory_space=pltpu.VMEM)


def smem():
    return pl.BlockSpec(memory_space=pltpu.SMEM)


def slot_scratch(extra):
    return (
        [pltpu.SMEM((8,), jnp.int32), pltpu.SMEM((1,), jnp.int32)]
        + extra
        + [
            pltpu.SMEM((48,), jnp.int32),
            pltpu.VMEM((2, 4 * LANES, 4 * LANES), BF16),
            pltpu.VMEM((MAXCOV, NVP, 64), BF16),
            pltpu.VMEM((MAXCOV, 32, NVP), BF16),
            pltpu.VMEM((9, 64, 2 * LANES), BF16),
            pltpu.VMEM((9, 32, 2 * LANES), BF16),
            pltpu.VMEM((9, 32, LANES), F32),
            pltpu.VMEM((8, 32, NVP), F32),
        ]
    )


def solvent_scratch(tiles):
    return [pltpu.VMEM((tiles * LANES, 64), BF16), pltpu.VMEM((32, 8 * LANES), F32)]


def call(kernel, outs, scratch, args, scalars=0):
    return pl.pallas_call(
        kernel,
        out_shape=tuple(jax.ShapeDtypeStruct(s, t) for s, t in outs),
        in_specs=[smem()] * scalars + [vmem()] * (len(args) - scalars),
        out_specs=tuple(vmem() for _ in outs),
        scratch_shapes=scratch,
    )(*args)


def moves(axis, shift):
    count = lax.axis_size(axis)
    return [(k, k + shift) for k in range(count) if 0 <= k + shift < count]


def swap(out_a, out_b):
    count = lax.axis_size("wa")
    odd_pairs = [(k, k - 1 if k % 2 == 0 else k + 1) for k in range(1, count - 1)]
    in_a = lax.ppermute(out_a, "wa", [(k, k ^ 1) for k in range(count)])
    return in_a, lax.ppermute(out_b, "wa", odd_pairs)


def columns(t0, t1, in_a, in_b):
    even = lax.axis_index("wa") % 2 == 0

    def column(f):
        a, b = in_a[:, f], in_b[:, f]
        return jnp.concatenate(
            [jnp.where(even, b, a), t0[:, f], t1[:, f], jnp.where(even, a, b)], 0
        )

    gl = lax.ppermute(column(TF - 1), "gx", moves("gx", 1))
    gh = lax.ppermute(column(0), "gx", moves("gx", -1))
    return gl, gh


def body(
    part_pos, part_vel, random_kicks, vert_pos, vert_vel,
    cover_start, bond_ends, triangles, rest_len, rest_area,
):
    cell = jnp.concatenate(
        [
            jnp.pad(vert_pos[:, 0], ((0, 0), (0, NVP - NV)), constant_values=FAR),
            jnp.pad(vert_vel[:, 0], ((0, 0), (0, NVP - NV))),
        ],
        0,
    )
    cell = jnp.transpose(cell.reshape(6, 4, LANES), (1, 0, 2)).reshape(24, LANES)
    tiles = jnp.transpose(
        jnp.concatenate([part_pos, part_vel, random_kicks[0:2]], 0), (1, 2, 0, 3)
    )
    t0, t1 = tiles[:1], tiles[1:]
    even = lax.axis_index("wa") % 2 == 0
    cell, t0, t1 = lax.optimization_barrier((cell, t0, t1))
    cells = lax.all_to_all(
        jnp.broadcast_to(cell[None], (SLABS, 24, LANES)), "gx", 0, 0, tiled=True
    )
    kicks = jnp.transpose(random_kicks[2:4], (1, 2, 0, 3))
    part = ((8, TW * TF * LANES), F32)
    row = ((1, TF, 8, LANES), F32)
    incidence, par = call(
        incidence_kernel,
        [((NVP, COLS), BF16), ((4, NBP), F32)],
        [pltpu.VMEM((8, SPAN * NBP), jnp.int32), pltpu.VMEM((8, SPAN * NBP), F32)],
        (bond_ends.T, triangles.T, rest_len[None], rest_area[None]),
    )
    sides = (jnp.where(even, t1, t0), jnp.where(even, t0, t1))
    swapped = swap(*sides)
    ends = columns(t0, t1, *swapped)
    (solv,) = call(early_kernel, [part], solvent_scratch(24), (t0, t1, *swapped, *ends))
    cell_scratch = pltpu.VMEM((8, 8, NVP), F32)
    n0, n1, n_a, n_b, cst, share = call(
        first_kernel,
        [row, row, row, row, ((48, NVP), F32), ((16, NVP), F32)],
        slot_scratch([cell_scratch]),
        (cover_start, t0, t1, kicks, cells, solv, incidence, par),
        1,
    )
    swapped = swap(n_a, n_b)
    got = []
    for shift in (-2, -1, 1, 2):
        got.append(lax.ppermute(share, "gx", moves("gx", -shift)))
    memb, sends = call(
        second_kernel,
        [part, ((SLABS, 24, LANES), F32)],
        slot_scratch(
            [pltpu.SMEM((4 * SLABS,), jnp.int32), cell_scratch, pltpu.VMEM((48, NVP), F32)]
        ),
        (cover_start, n0, n1, cst, share, *got, incidence, par),
        1,
    )
    final = jnp.sum(lax.all_to_all(sends, "gx", 0, 0, tiled=True), 0)
    ends = columns(n0, n1, *swapped)
    (inner,) = call(inner_kernel, [part], solvent_scratch(8), (n0, n1, memb))
    out_pos, out_vel = call(
        late_kernel,
        [((3, TW, TF, LANES), F32)] * 2,
        solvent_scratch(16),
        (n0, n1, *swapped, *ends, inner),
    )
    final = jnp.transpose(final.reshape(4, 6, LANES), (1, 0, 2)).reshape(6, NVP)
    new_vel = final[3:6, None, :NV]
    new_pos = final[0:3, None, :NV] + DT * new_vel
    return out_pos, out_vel, new_pos, new_vel


def solution(mesh):
    in_specs = (
        P(None, "wa", "gx", None),
        P(None, "wa", "gx", None),
        P(None, "wa", "gx", None),
        P(None, ("wa", "gx"), None),
        P(None, ("wa", "gx"), None),
        P("wa"),
        P(),
        P(),
        P(),
        P(),
    )
    out_specs = (
        P(None, "wa", "gx", None),
        P(None, "wa", "gx", None),
        P(None, ("wa", "gx"), None),
        P(None, ("wa", "gx"), None),
    )
    return jax.shard_map(body, mesh=mesh, in_specs=in_specs, out_specs=out_specs, check_vma=False)
```
